32 devices in a mesh: cannon: 8 (over y, x, core), rep: 4 (over z).
Axes of the slice: x: 2, y: 2, z: 4, core: 2. Of those that a mesh axis runs over, the one named last changes fastest.
Arguments:
- root_margin: bfloat16 [32, 8, 128, 128], P('cannon', 'rep'), may hold values from -2.5 to 2.5
- inverse_root: bfloat16 [32, 8, 128, 128], P('cannon', 'rep'), may hold values from -2.5 to 2.5
- hamiltonian: bfloat16 [32, 8, 128, 128], P('cannon', 'rep'), may hold values from -0.25 to 0.25
- margin_mask: int32 [32, 8], P('cannon', 'rep'), may hold values from 0 to 1, as said below
- hamilton_mask: int32 [32, 8], P('cannon', 'rep'), may hold values from 0 to 1, as said below
Outputs:
- root_next: bfloat16 [32, 8, 128, 128], P('cannon', 'rep')
- inverse_next: bfloat16 [32, 8, 128, 128], P('cannon', 'rep')
- lowdin_product: bfloat16 [32, 8, 128, 128], P('cannon', 'rep')
The draws below stay inside these ranges and needn't reach their ends.
Inputs may be any that keep to these rules, and one draw needn't show every extreme that they name: `margin_mask`: 0 or 1; slot 8 // 2 (the diagonal block) is 1 in every block row; all block rows of one index of cannon share a fill level drawn from the seed, from one eighth to full. `hamilton_mask`: 0 or 1; slot 8 // 2 (the diagonal block) is 1 in every block row; all block rows of one index of cannon share a fill level drawn from the seed, from one eighth to full.
All inputs are finite; a program needn't handle non-finite values.
Results may differ from the reference program's by a relative error of at most 0.018.
Values may be sent and summed in bfloat16 or wider, within the bound.
No kernel may reach another device: no remote copies, remote signals or barrier semaphores. Data moves between devices by JAX's collectives and lax.ppermute only.
A program may use at most 64 MiB of HBM per device.

```python
import jax
import jax.numpy as jnp
from jax import lax

BLK = 128
NS = 8
BR_DEV = 4
NB = 32
N_REP = 4


def pattern_draw(key):
    panels = NB // BR_DEV
    fill_level = jax.random.randint(jax.random.fold_in(key, 11), (panels, 1), 1, 9)
    fill_level = jnp.repeat(fill_level, BR_DEV, axis=0)
    random_picks = jax.random.randint(jax.random.fold_in(key, 12), (NB, NS), 0, 8)
    pattern = (random_picks < fill_level).astype(jnp.int32)
    diagonal = (jnp.arange(NS) == NS // 2)[None, :]
    return jnp.where(diagonal, 1, pattern).astype(jnp.int32)


def draw_margin_mask(key, part):
    return pattern_draw(jax.random.fold_in(key, 1))


def draw_hamilton_mask(key, part):
    return pattern_draw(jax.random.fold_in(key, 2))


def block_levels(rng, extent, pieces, least, largest):
    factor_of, own = 1.0, jax.random.fold_in(rng, 6)
    for dim, parts in pieces:
        heights = jnp.exp(jax.random.uniform(jax.random.fold_in(own, dim), (parts,), jnp.float32, least / len(pieces), largest / len(pieces)))
        factor_of = factor_of * jnp.repeat(heights, extent[dim] // parts).reshape([-1 if axis == dim else 1 for axis in range(len(extent))])
    return factor_of


def centred(key, extent, deviation, bound, cuts=(), kind=jnp.bfloat16):
    result = deviation * jax.random.normal(key, extent, jnp.float32)
    if cuts:
        result = result * block_levels(key, extent, cuts, -0.22, 0.18)
    return jnp.clip(result, -bound, bound).astype(kind)


def setup_inputs(seed: int = 0) -> dict:
    streams_of = jax.random.split(jax.random.key(seed), 6)
    root_margin = centred(streams_of[0], (NB, NS, BLK, BLK), ((BLK * NS) ** -0.25), 2.5, ((0, 8), (1, 4)))
    inverse_root = centred(streams_of[1], (NB, NS, BLK, BLK), ((BLK * NS) ** -0.25), 2.5, ((0, 8), (1, 4)))
    hamiltonian = centred(streams_of[2], (NB, NS, BLK, BLK), (0.6 / (BLK * NS) ** 0.5), 0.25, ((0, 8), (1, 4)))
    margin_mask = draw_margin_mask(jax.random.fold_in(streams_of[5], 71), 0)
    hamilton_mask = draw_hamilton_mask(jax.random.fold_in(streams_of[5], 71), 0)
    return dict(root_margin=root_margin, inverse_root=inverse_root, hamiltonian=hamiltonian, margin_mask=margin_mask, hamilton_mask=hamilton_mask)


def band_product(first_factor, second_factor, pattern):
    slot_count = first_factor.shape[1]
    half_band = slot_count // 2
    group_slots = slot_count // N_REP
    summed = jnp.zeros(first_factor.shape, jnp.float32)
    for replica in range(N_REP):
        partial_value = jnp.zeros(first_factor.shape, jnp.float32)
        for offset in range(replica * group_slots, (replica + 1) * group_slots):
            shifted = jnp.roll(second_factor, half_band - offset, axis=0)
            first_slot = max(0, offset - half_band)
            last_slot = min(slot_count, offset + half_band)
            addend = jnp.einsum("ipq,itqr->itpr", first_factor[:, offset].astype(jnp.float32),
                                shifted[:, first_slot - offset + half_band:last_slot - offset + half_band].astype(jnp.float32))
            partial_value = partial_value.at[:, first_slot:last_slot].add(addend)
        summed = summed + lax.optimization_barrier(partial_value.astype(jnp.bfloat16)).astype(jnp.float32)
    return summed * pattern[:, :, None, None].astype(jnp.float32)


def reference(root_margin, inverse_root, hamiltonian, margin_mask, hamilton_mask):
    margin_scale = margin_mask[:, :, None, None].astype(jnp.bfloat16)
    hamilton_scale = hamilton_mask[:, :, None, None].astype(jnp.bfloat16)
    root_masked = root_margin * margin_scale
    inverse_masked = inverse_root * margin_scale
    hamilton_masked = hamiltonian * hamilton_scale
    product = band_product(inverse_masked, root_masked, margin_mask)
    slot_ids = jnp.arange(NS)
    diagonal = (slot_ids == NS // 2).astype(jnp.float32)[None, :, None, None] * jnp.eye(BLK, dtype=jnp.float32)[None, None]
    polynomial = (1.5 * diagonal - 0.5 * product).astype(jnp.bfloat16)
    inverse_next = band_product(polynomial, inverse_masked, margin_mask).astype(jnp.bfloat16)
    root_next = band_product(root_masked, polynomial, margin_mask).astype(jnp.bfloat16)
    lowdin_product = band_product(inverse_next, hamilton_masked, hamilton_mask).astype(jnp.bfloat16)
    return root_next, inverse_next, lowdin_product
```

```python
import functools

import jax
import jax.numpy as jnp
from jax import lax
from jax.experimental import pallas as pl
from jax.experimental.pallas import tpu as pltpu
from jax.sharding import PartitionSpec as P

VMEM_LIMIT = 56 * 1024 * 1024
AXES = ("cannon", "rep")


class Plan:
    def __init__(self, rows, group, groups, block, cannon):
        slots = group * groups
        half = slots // 2
        assert rows >= half and cannon % 2 == 0
        self.n, self.g, self.G, self.S, self.hb, self.b = rows, group, groups, slots, half, block
        self.C = cannon
        self.mask_rows = -(-rows * group // 16) * 16
        self.unit = rows * group * block + self.mask_rows
        self.width = 3 * rows + slots - 1
        self.span = rows + slots - 1
        self.steps = groups - 1
        self.near = min(groups - 1, (half + group - 1) // group)
        full_up, full_dn = set(), set()
        wide = [(set(), set()) for _ in range(groups)]
        for i in range(rows):
            for t in range(slots):
                for s in range(slots):
                    u = t - s + half
                    k = i + s - half
                    if not 0 <= u < slots:
                        continue
                    if k < 0:
                        full_up.add((k + rows, u))
                        wide[t // group][0].add((k + rows, u))
                    elif k >= rows:
                        full_dn.add((k - rows, u))
                        wide[t // group][1].add((k - rows, u))
        self.full = (sorted(full_up), sorted(full_dn))
        self.wide = [(sorted(a), sorted(b)) for a, b in wide]
        self.full_len = max(len(x) for x in self.full)
        self.wide_len = max(len(x) for w in self.wide for x in w)

    def positions(self, lists):
        out = []
        for z in range(self.G):
            for kind in range(2):
                row = [-1] * (self.n * self.S)
                for at, (r, u) in enumerate(lists[z][kind]):
                    row[r * self.S + u] = at
                out += row
        return jnp.asarray(out, jnp.int32)

    def entries(self):
        out = []
        for z in range(self.G):
            for kind in range(2):
                row = [r * self.S + u for r, u in self.wide[z][kind]]
                out += row + [-1] * (self.wide_len - len(row))
        return jnp.asarray(out, jnp.int32)


def place_of():
    par = lax.rem(lax.axis_index("cannon"), 2)
    return par, lax.axis_index("rep")


def at(index, block):
    if isinstance(index, int):
        return pl.ds(index * block, block)
    return pl.ds(pl.multiple_of(index * block, block), block)


def prep_kernel(p, r_ref, i_ref, h_ref, mm_ref, hm_ref, rp_ref, ip_ref, hp_ref):
    b = p.b
    for out in (rp_ref, ip_ref, hp_ref):
        out[p.n * p.g * b :, :] = jnp.zeros((p.mask_rows, b), jnp.bfloat16)
    rows = lax.broadcasted_iota(jnp.int32, (p.mask_rows, b), 0)
    margin = jnp.zeros((p.mask_rows, b), jnp.float32)
    hamilton = jnp.zeros((p.mask_rows, b), jnp.float32)
    for r in range(p.n):
        for e in range(p.g):
            m = (mm_ref[e, r] > 0).astype(jnp.float32)
            h = (hm_ref[e, r] > 0).astype(jnp.float32)
            block = pl.ds((r * p.g + e) * b, b)
            rp_ref[block, :] = (r_ref[r, e].astype(jnp.float32) * m).astype(jnp.bfloat16)
            ip_ref[block, :] = (i_ref[r, e].astype(jnp.float32) * m).astype(jnp.bfloat16)
            hp_ref[block, :] = (h_ref[r, e].astype(jnp.float32) * h).astype(jnp.bfloat16)
            margin = jnp.where(rows == r * p.g + e, m, margin)
            hamilton = jnp.where(rows == r * p.g + e, h, hamilton)
    rp_ref[p.n * p.g * b :, :] = margin.astype(jnp.bfloat16)
    hp_ref[p.n * p.g * b :, :] = hamilton.astype(jnp.bfloat16)


def vmem(count):
    return [pl.BlockSpec(memory_space=pltpu.VMEM)] * count


def smem(count):
    return [pl.BlockSpec(memory_space=pltpu.SMEM)] * count


def params():
    return pltpu.CompilerParams(vmem_limit_bytes=VMEM_LIMIT)


def prep(p, root, inverse, hamilton, margin_mask, hamilton_mask):
    out = jax.ShapeDtypeStruct((p.unit, p.b), jnp.bfloat16)
    return pl.pallas_call(
        functools.partial(prep_kernel, p),
        out_shape=(out, out, out),
        in_specs=vmem(3) + smem(2),
        out_specs=tuple(vmem(3)),
        compiler_params=params(),
        name="prep",
    )(root, inverse, hamilton, margin_mask.T, hamilton_mask.T)


def each_piece(p, pieces, steps, visit):
    par, z = place_of()
    sign = 1 - 2 * par
    own, partner, held, swapped = pieces
    visit(own, True, z)
    visit(partner, False, z)
    for s in range(1, steps + 1):
        for refs, group, order in ((held, z - sign * s, (True, False)), (swapped, z + sign * s, (False, True))):

            @pl.when((group >= 0) & (group < p.G))
            def _():
                for half in range(2):
                    visit(refs[s - 1].at[half], order[half], group)


def split(refs, steps):
    return refs[0], refs[1], refs[2 : 2 + steps], refs[2 + steps : 2 + 2 * steps]


def pack_kernel(p, steps, *refs):
    table, refs, out = refs[0], refs[1:-1], refs[-1]
    par, z = place_of()
    base = (z * 2 + (1 - par)) * (p.n * p.S)

    def visit(ref, own, group):
        if not own:
            return
        for r in range(p.n):
            for e in range(p.g):
                to = table[base + r * p.S + p.g * group + e]

                @pl.when(to >= 0)
                def _():
                    out[to] = ref[pl.ds((r * p.g + e) * p.b, p.b), :]

    each_piece(p, split(refs, steps), steps, visit)


def pack(p, pieces, steps, lists, length):
    own, partner, held, swapped = pieces
    args = [own, partner, *held, *swapped]
    return pl.pallas_call(
        functools.partial(pack_kernel, p, steps),
        out_shape=jax.ShapeDtypeStruct((length, p.b, p.b), jnp.bfloat16),
        in_specs=smem(1) + vmem(len(args)),
        out_specs=vmem(1)[0],
        compiler_params=params(),
        name="pack",
    )(p.positions(lists), *args)


def clear_outside(p, dense):
    lo, hi = p.n, p.n + p.span
    for k in range(p.n - p.hb, 2 * p.n + p.hb - 1):
        left, right = max(lo, min(hi, k)), min(hi, k + p.S)
        if left > lo:
            dense[at(k, p.b), lo * p.b : left * p.b] = jnp.zeros((p.b, (left - lo) * p.b), jnp.bfloat16)
        if right < hi:
            dense[at(k, p.b), right * p.b : hi * p.b] = jnp.zeros((p.b, (hi - right) * p.b), jnp.bfloat16)


def fill(p, dense, pieces, steps, own_only=False):
    par, _ = place_of()
    aside = p.n + p.n * (1 - 2 * par)

    def visit(ref, own, group):
        if own_only and not own:
            return
        for r in range(p.n):
            k = p.n + r if own else aside + r
            for e in range(p.g):
                dense[at(k, p.b), at(k + p.g * group + e, p.b)] = ref[pl.ds((r * p.g + e) * p.b, p.b), :]

    each_piece(p, pieces, steps, visit)


def fill_full(p, dense, message):
    par, _ = place_of()
    for kind, base in ((0, 0), (1, 2 * p.n)):

        @pl.when(par == kind)
        def _():
            for m, (r, u) in enumerate(p.full[kind]):
                dense[at(base + r, p.b), at(base + r + u, p.b)] = message[m]


def fill_wide(p, dense, message, table, kind):
    _, z = place_of()
    base = kind * 2 * p.n

    @pl.loop(0, p.wide_len)
    def _(m):
        code = table[(z * 2 + kind) * p.wide_len + m]

        @pl.when(code >= 0)
        def _():
            k = base + lax.div(code, p.S)
            dense[at(k, p.b), at(k + lax.rem(code, p.S), p.b)] = message[m]


def send_wide(p, dense_rows, out, table, kind):
    _, z = place_of()

    @pl.loop(0, p.wide_len)
    def _(m):
        code = table[(z * 2 + kind) * p.wide_len + m]

        @pl.when(code >= 0)
        def _():
            r = lax.div(code, p.S)
            out[m] = dense_rows[at(r, p.b), at(r + lax.rem(code, p.S), p.b)]


def band_matmul(p, rows, dense, finish):
    b = p.b
    lo, hi = p.n, p.n + p.span
    for c0 in range(lo, hi, 2):
        c1 = min(c0 + 2, hi)
        k0 = max(c0 - p.S + 1, p.n - p.hb)
        k1 = min(c1 - 1, 2 * p.n + p.hb - 2) + 1
        value = jnp.dot(
            rows[:, (k0 + p.hb - p.n) * b : (k1 + p.hb - p.n) * b],
            dense[k0 * b : k1 * b, c0 * b : c1 * b],
            preferred_element_type=jnp.float32,
        )
        for c in range(c0, c1):
            for i in range(p.n):
                t = c - p.n - i
                finish(i, t if 0 <= t < p.S else None, c - p.n, value[i * b : (i + 1) * b, (c - c0) * b : (c - c0 + 1) * b])


def mask_of(p, marks, i, t):
    return marks[t // p.g, i * p.g + t % p.g : i * p.g + t % p.g + 1, :]


def polynomial_kernel(p, *refs):
    count = 2 + 2 * p.steps
    table, message = refs[0], refs[1]
    root = split(refs[2 : 2 + count], p.steps)
    inverse = split(refs[2 + count : 2 + 2 * count], p.steps)
    poly, across, aside, rows_out, marks = refs[2 + 2 * count : 7 + 2 * count]
    dense, left = refs[7 + 2 * count :]
    b = p.b
    par, z = place_of()
    clear_outside(p, dense)
    fill(p, dense, root, p.steps)
    fill_full(p, dense, message)
    left[...] = jnp.zeros_like(left)

    def visit(ref, own, group):
        if not own:
            return
        for r in range(p.n):
            for e in range(p.g):
                left[at(r, b), at(r + p.g * group + e, b)] = inverse_block(ref, r, e)

    def inverse_block(ref, r, e):
        return ref[pl.ds((r * p.g + e) * b, b), :]

    each_piece(p, inverse, p.steps, visit)

    def note(ref, own, group):
        if own:
            marks[group] = ref[p.n * p.g * b : p.unit, :].astype(jnp.float32)

    each_piece(p, root, p.steps, note)
    rows_out[...] = dense[p.n * b : 2 * p.n * b, p.n * b : (p.n + p.span) * b]
    eye = (
        lax.broadcasted_iota(jnp.int32, (b, b), 0) == lax.broadcasted_iota(jnp.int32, (b, b), 1)
    ).astype(jnp.float32)

    def finish(i, t, column, value):
        if t is None:
            poly[at(i, b), at(column, b)] = jnp.zeros((b, b), jnp.bfloat16)
            return
        value = -0.5 * (value * mask_of(p, marks, i, t))
        if t == p.hb:
            value = 1.5 * eye + value
        poly[at(i, b), at(column, b)] = value.astype(jnp.bfloat16)

    band_matmul(p, left, dense, finish)
    for kind in range(2):

        @pl.when(par == kind)
        def _():
            send_wide(p, poly, across, table, 1 - kind)
            send_wide(p, poly, aside, table, kind)


def polynomial(p, table, message, root, inverse):
    args = [root[0], root[1], *root[2], *root[3], inverse[0], inverse[1], *inverse[2], *inverse[3]]
    b = p.b
    wide = jax.ShapeDtypeStruct((p.wide_len, b, b), jnp.bfloat16)
    dense = jax.ShapeDtypeStruct((p.n * b, p.span * b), jnp.bfloat16)
    return pl.pallas_call(
        functools.partial(polynomial_kernel, p),
        out_shape=(dense, wide, wide, dense, jax.ShapeDtypeStruct((p.G, p.mask_rows, b), jnp.float32)),
        in_specs=smem(1) + vmem(1 + len(args)),
        out_specs=tuple(vmem(5)),
        scratch_shapes=[
            pltpu.VMEM((3 * p.n * b, p.width * b), jnp.bfloat16),
            pltpu.VMEM((p.n * b, p.span * b), jnp.bfloat16),
        ],
        compiler_params=params(),
        name="polynomial",
    )(table, message, *args)


def row_matmul(p, rows, dense, i, z):
    b = p.b
    return jnp.dot(
        rows[i * b : (i + 1) * b, i * b : (i + p.S) * b],
        dense[(p.n + i - p.hb) * b : (p.n + i + p.hb) * b, pl.ds(pl.multiple_of((p.n + i + p.g * z) * b, b), p.g * b)],
        preferred_element_type=jnp.float32,
    )


def outputs_kernel(p, *refs):
    full, near = 2 + 2 * p.steps, 2 + 2 * p.near
    table, poly, poly_across, poly_aside, rows, marks, root_own = refs[:7]
    refs = refs[7:]
    message, hamilton_message = refs[:2]
    inverse = split(refs[2 : 2 + full], p.steps)
    hamilton = split(refs[2 + full : 2 + full + near], p.near)
    root_out, inverse_out, lowdin_out, dense, band, next_rows = refs[2 + full + near :]
    b = p.b
    par, z = place_of()

    clear_outside(p, band)
    band[p.n * b : 2 * p.n * b, p.n * b : (p.n + p.span) * b] = poly[...]
    for kind in range(2):

        @pl.when(par == kind)
        def _():
            fill_wide(p, band, poly_across, table, kind)
            fill_wide(p, band, poly_aside, table, 1 - kind)

    own_marks = root_own[p.n * p.g * b : p.unit, :].astype(jnp.float32)
    for i in range(p.n):
        value = row_matmul(p, rows, band, i, z)
        for e in range(p.g):
            m = own_marks[i * p.g + e : i * p.g + e + 1, :]
            root_out[i, e] = (value[:, e * b : (e + 1) * b] * m).astype(jnp.bfloat16)

    clear_outside(p, dense)
    fill(p, dense, inverse, p.steps)
    fill_full(p, dense, message)

    def finish(i, t, column, value):
        if t is not None:
            next_rows[at(i, b), at(column, b)] = (value * mask_of(p, marks, i, t)).astype(jnp.bfloat16)

    band_matmul(p, poly, dense, finish)
    for i in range(p.n):
        for e in range(p.g):
            inverse_out[i, e] = next_rows[at(i, b), at(i + p.g * z + e, b)]

    clear_outside(p, band)
    fill(p, band, hamilton, p.near)
    for kind in range(2):

        @pl.when(par == kind)
        def _():
            fill_wide(p, band, hamilton_message, table, kind)

    own_marks = hamilton[0][p.n * p.g * b : p.unit, :].astype(jnp.float32)
    for i in range(p.n):
        value = row_matmul(p, next_rows, band, i, z)
        for e in range(p.g):
            m = own_marks[i * p.g + e : i * p.g + e + 1, :]
            lowdin_out[i, e] = (value[:, e * b : (e + 1) * b] * m).astype(jnp.bfloat16)


def outputs(p, table, poly, poly_across, poly_aside, rows, marks, message, hamilton_message, root_own, inverse, hamilton):
    args = [poly, poly_across, poly_aside, rows, marks, root_own, message, hamilton_message]
    for op in (inverse, hamilton):
        args += [op[0], op[1], *op[2], *op[3]]
    b = p.b
    out = jax.ShapeDtypeStruct((p.n, p.g, b, b), jnp.bfloat16)
    return pl.pallas_call(
        functools.partial(outputs_kernel, p),
        out_shape=(out, out, out),
        in_specs=smem(1) + vmem(len(args)),
        out_specs=tuple(vmem(3)),
        scratch_shapes=[
            pltpu.VMEM((3 * p.n * b, p.width * b), jnp.bfloat16),
            pltpu.VMEM((3 * p.n * b, p.width * b), jnp.bfloat16),
            pltpu.VMEM((p.n * b, p.span * b), jnp.bfloat16),
        ],
        compiler_params=params(),
        name="outputs",
    )(table, *args)


def body(root_margin, inverse_root, hamiltonian, margin_mask, hamilton_mask):
    rows, group, block = root_margin.shape[0], root_margin.shape[1], root_margin.shape[2]
    groups, cannon = lax.axis_size("rep"), lax.axis_size("cannon")
    p = Plan(rows, group, groups, block, cannon)

    relay_route = []
    for c in range(cannon):
        for z in range(groups):
            to = z + 1 if c % 2 == 0 else z - 1
            if 0 <= to < groups:
                relay_route.append((c * groups + z, c * groups + to))
    aside_route = [(c, c ^ 1) for c in range(cannon)]
    across_route = [(c, (c + 1) % cannon if c % 2 else (c - 1) % cannon) for c in range(cannon)]

    def relay(x):
        return lax.ppermute(x, AXES, relay_route)

    def aside(x):
        return lax.ppermute(x, "cannon", aside_route)

    def across(x):
        return lax.ppermute(x, "cannon", across_route)

    own = prep(p, root_margin, inverse_root, hamiltonian, margin_mask, hamilton_mask)
    partner = [aside(x) for x in own]
    held = {}
    order = [(0, 1), (1, 1), (0, 2), (2, 1), (0, 3), (1, 2), (2, 2), (1, 3)]
    limit = (p.steps, p.steps, p.near)
    order = [(o, s) for o, s in order if s <= limit[o]]
    order += [(o, s) for o in range(3) for s in range(1, limit[o] + 1) if (o, s) not in order]
    for o, s in order:
        held[o, s] = relay(jnp.stack([own[o], partner[o]]) if s == 1 else held[o, s - 1])
    pieces = []
    for o in range(3):
        mine = [held[o, s] for s in range(1, limit[o] + 1)]
        pieces.append((own[o], partner[o], mine, [aside(x) for x in mine]))
    root, inverse, hamilton = pieces
    full = [p.full] * p.G
    table = p.entries()
    root_message = across(pack(p, root, p.steps, full, p.full_len))
    inverse_message = across(pack(p, inverse, p.steps, full, p.full_len))
    hamilton_message = across(pack(p, hamilton, p.near, p.wide, p.wide_len))
    poly, poly_across, poly_aside, root_rows, marks = polynomial(p, table, root_message, root, inverse)
    poly_across = across(poly_across)
    poly_aside = aside(poly_aside)
    return outputs(
        p, table, poly, poly_across, poly_aside, root_rows, marks, inverse_message, hamilton_message, own[0], inverse, hamilton
    )


def solution(mesh):
    blocks = P("cannon", "rep", None, None)
    masks = P("cannon", "rep")
    return jax.shard_map(
        body,
        mesh=mesh,
        in_specs=(blocks, blocks, blocks, masks, masks),
        out_specs=(blocks, blocks, blocks),
        check_vma=False,
    )
```

```python
import functools

import jax
import jax.numpy as jnp
from jax import lax
from jax.experimental import pallas as pl
from jax.experimental.pallas import tpu as pltpu
from jax.sharding import PartitionSpec as P


VMEM_LIMIT = 22 * 1024 * 1024
AXES = ("cannon", "rep")


class Plan:
    def __init__(self, rows, group, groups, block, cannon):
        slots = group * groups
        half = slots // 2
        assert rows >= half and cannon % 2 == 0
        self.n, self.g, self.G, self.S, self.hb, self.b = rows, group, groups, slots, half, block
        self.mask_rows = -(-rows * group // 16) * 16
        self.unit = rows * group * block + self.mask_rows
        self.width = 3 * rows + slots - 1
        self.span = rows + slots - 1
        self.steps = groups - 1
        full_up, full_dn = set(), set()
        for i in range(rows):
            for t in range(slots):
                for s in range(slots):
                    u = t - s + half
                    k = i + s - half
                    if not 0 <= u < slots:
                        continue
                    if k < 0:
                        full_up.add((k + rows, u))
                    elif k >= rows:
                        full_dn.add((k - rows, u))
        for r in range(rows):
            for s in range(slots):
                if 0 <= r - rows + s - half < rows:
                    full_up.add((r, s))
                if 0 <= r + rows + s - half < rows:
                    full_dn.add((r, s))
        self.full = (sorted(full_up), sorted(full_dn))

        def needed(away):
            found = set()
            for i in range(rows):
                for e_out in range(group):
                    for e in range(group):
                        shift = group * away + e_out - e
                        if 0 <= shift + half < slots:
                            found.add((i + shift, e))
            return found

        self.near = max([d for d in range(1, groups) if needed(d) or needed(-d)], default=0)
        self.ahead, self.behind = {}, {}
        for lists, sign in ((self.ahead, 1), (self.behind, -1)):
            so_far = []
            for d in range(self.near, 0, -1):
                so_far = so_far + sorted(needed(sign * d) - set(so_far))
                lists[d] = so_far
        self.near_len = {d: max(len(self.ahead[d]), len(self.behind[d])) for d in range(1, self.near + 1)}

    def halo(self, steps):
        out = []
        for z in range(self.G):
            kinds = []
            for kind in range(2):
                kinds.append([(r, u) for r, u in self.full[kind] if abs(u // self.g - z) in steps])
            out.append(kinds)
        return out

    def halo_split(self, own, least):
        early, late = self.halo(range(0 if own else 1, self.steps)), self.halo([self.steps])
        total = max(len(a) + len(b) for x, y in zip(early, late) for a, b in zip(x, y))
        size = min(least, total - self.length(late)) if least else total - self.length(late)
        first = [[kind[:size] for kind in kinds] for kinds in early]
        rest = [[b + a[size:] for a, b in zip(x, y)] for x, y in zip(early, late)]
        return first, rest

    def length(self, lists):
        return max(len(x) for kinds in lists for x in kinds)

    def positions(self, lists):
        out = []
        for z in range(self.G):
            for kind in range(2):
                row = [-1] * (self.n * self.S)
                for at, (r, u) in enumerate(lists[z][kind]):
                    row[r * self.S + u] = at
                out += row
        return jnp.asarray(out, jnp.int32)

    def entries(self, lists):
        length = self.length(lists)
        out = []
        for z in range(self.G):
            for kind in range(2):
                row = [r * self.S + u for r, u in lists[z][kind]]
                out += row + [-1] * (length - len(row))
        return jnp.asarray(out, jnp.int32)


def place_of():
    par = lax.rem(lax.axis_index("cannon"), 2)
    return par, lax.axis_index("rep")


def at(index, block):
    if isinstance(index, int):
        return pl.ds(index * block, block)
    return pl.ds(pl.multiple_of(index * block, block), block)


def prep_kernel(p, x_ref, mask_ref, out_ref, staged, done):
    b = p.b
    copy = pltpu.make_async_copy(x_ref, staged, done)
    copy.start()
    rows = lax.broadcasted_iota(jnp.int32, (p.mask_rows, b), 0)
    marks = jnp.zeros((p.mask_rows, b), jnp.float32)
    values = []
    for r in range(p.n):
        for e in range(p.g):
            m = (mask_ref[e, r] > 0).astype(jnp.float32)
            values.append(m)
            marks = jnp.where(rows == r * p.g + e, m, marks)
    out_ref[p.n * p.g * b :, :] = marks.astype(jnp.bfloat16)
    copy.wait()
    for r in range(p.n):
        for e in range(p.g):
            value = staged[r, e].astype(jnp.float32) * values[r * p.g + e]
            out_ref[pl.ds((r * p.g + e) * b, b), :] = value.astype(jnp.bfloat16)


def vmem(count):
    return [pl.BlockSpec(memory_space=pltpu.VMEM)] * count


def smem(count):
    return [pl.BlockSpec(memory_space=pltpu.SMEM)] * count


def params(limit=VMEM_LIMIT):
    return pltpu.CompilerParams(vmem_limit_bytes=limit)


def prep(p, x, mask):
    return pl.pallas_call(
        functools.partial(prep_kernel, p),
        out_shape=jax.ShapeDtypeStruct((p.unit, p.b), jnp.bfloat16),
        in_specs=[pl.BlockSpec(memory_space=pltpu.HBM)] + smem(1),
        out_specs=vmem(1)[0],
        scratch_shapes=[pltpu.VMEM((p.n, p.g, p.b, p.b), jnp.bfloat16), pltpu.SemaphoreType.DMA(())],
        compiler_params=params(),
        name="prep",
    )(x, mask.T)


def each_piece(p, pieces, steps, visit):
    par, z = place_of()
    sign = 1 - 2 * par
    own, partner, held, swapped = pieces
    if own is not None:
        visit(own, True, z)
        visit(partner, False, z)
    for m, s in enumerate(steps):
        for refs, group, order in ((held, z - sign * s, (True, False)), (swapped, z + sign * s, (False, True))):

            @pl.when((group >= 0) & (group < p.G))
            def _():
                for half in range(2):
                    visit(refs[m].at[half], order[half], group)


def split(refs, steps):
    return refs[0].at[0], refs[0].at[1], refs[1 : 1 + steps], refs[1 + steps : 1 + 2 * steps]


def pack_kernel(p, steps, with_own, *refs):
    table, refs, out = refs[0], refs[1:-1], refs[-1]
    par, z = place_of()
    base = (z * 2 + (1 - par)) * (p.n * p.S)

    def visit(ref, own, group):
        if not own:
            return
        for r in range(p.n):
            for e in range(p.g):
                to = table[base + r * p.S + p.g * group + e]

                @pl.when(to >= 0)
                def _():
                    out[to] = ref[pl.ds((r * p.g + e) * p.b, p.b), :]

    if with_own:
        pieces = split(refs, len(steps))
    else:
        pieces = (None, None, refs[: len(steps)], refs[len(steps) :])
    each_piece(p, pieces, steps, visit)


def pack(p, pieces, steps, with_own, lists):
    both, held, swapped = pieces
    args = [both] if with_own else []
    args += [held[s - 1] for s in steps] + [swapped[s - 1] for s in steps]
    return pl.pallas_call(
        functools.partial(pack_kernel, p, steps, with_own),
        out_shape=jax.ShapeDtypeStruct((p.length(lists), p.b, p.b), jnp.bfloat16),
        in_specs=smem(1) + vmem(len(args)),
        out_specs=vmem(1)[0],
        compiler_params=params(),
        name="pack",
    )(p.positions(lists), *args)


def pack_near_kernel(p, own, partner, beyond, out):
    par, _ = place_of()
    for kind, blocks in ((0, p.ahead[1]), (1, p.behind[1])):

        @pl.when(par == kind)
        def _():
            for m, (k, e) in enumerate(blocks):
                inside = 0 <= k < p.n
                r = k % p.n
                at_row = pl.ds((r * p.g + e) * p.b, p.b)
                out[0, m] = (own if inside else partner)[at_row, :]
                out[1, m] = (partner if inside else beyond)[at_row, :]


def pack_near(p, own, partner, beyond):
    return pl.pallas_call(
        functools.partial(pack_near_kernel, p),
        out_shape=jax.ShapeDtypeStruct((2, p.near_len[1], p.b, p.b), jnp.bfloat16),
        in_specs=vmem(3),
        out_specs=vmem(1)[0],
        compiler_params=params(),
        name="pack_near",
    )(own, partner, beyond)


def trim_kernel(x_ref, out_ref):
    out_ref[...] = x_ref[:, : out_ref.shape[1]]


def trim(p, x, length):
    return pl.pallas_call(
        trim_kernel,
        out_shape=jax.ShapeDtypeStruct((2, length, p.b, p.b), jnp.bfloat16),
        in_specs=vmem(1),
        out_specs=vmem(1)[0],
        compiler_params=params(),
        name="trim",
    )(x)


def clear_outside(p, dense):
    lo, hi = p.n, p.n + p.span
    for k in range(3 * p.n):
        left, right = max(lo, min(hi, k)), min(hi, k + p.S)
        if left > lo:
            dense[at(k, p.b), lo * p.b : left * p.b] = jnp.zeros((p.b, (left - lo) * p.b), jnp.bfloat16)
        if right < hi:
            dense[at(k, p.b), right * p.b : hi * p.b] = jnp.zeros((p.b, (hi - right) * p.b), jnp.bfloat16)


def fill(p, dense, pieces, steps, own_only=False):
    par, _ = place_of()
    aside = p.n + p.n * (1 - 2 * par)

    def visit(ref, own, group):
        if own_only and not own:
            return
        for r in range(p.n):
            k = p.n + r if own else aside + r
            for e in range(p.g):
                dense[at(k, p.b), at(k + p.g * group + e, p.b)] = ref[pl.ds((r * p.g + e) * p.b, p.b), :]

    each_piece(p, pieces, steps, visit)


def fill_halo(p, dense, message, table):
    par, z = place_of()
    length = message.shape[0]

    @pl.loop(0, length)
    def _(m):
        code = table[(z * 2 + par) * length + m]

        @pl.when(code >= 0)
        def _():
            k = par * (2 * p.n) + lax.div(code, p.S)
            dense[at(k, p.b), at(k + lax.rem(code, p.S), p.b)] = message[m]


def fill_own(p, dense, ref, base, group):
    for r in range(p.n):
        for e in range(p.g):
            dense[at(base + r, p.b), at(base + r + p.g * group + e, p.b)] = row_blocks(ref, r, e, p)


def fill_near(p, dense, own, partner, beyond, held, swapped):
    par, z = place_of()
    sign = 1 - 2 * par
    for ref, base in ((own, p.n), (partner, p.n + p.n * sign), (beyond, par * (2 * p.n))):
        fill_own(p, dense, ref, base, z)
    for s in range(1, p.near + 1):
        for kind, first, second in ((0, p.ahead[s], p.behind[s]), (1, p.behind[s], p.ahead[s])):
            for refs, part, blocks, group in (
                (held, 0, first, z - sign * s),
                (swapped, 1, second, z + sign * s),
            ):

                @pl.when((par == kind) & (group >= 0) & (group < p.G))
                def _():
                    for m, (k, e) in enumerate(blocks):
                        dense[at(k + p.n, p.b), at(k + p.n + p.g * group + e, p.b)] = refs[s - 1][part, m]


def band_matmul(p, rows, dense, finish):
    b = p.b
    lo, hi = p.n, p.n + p.span
    for c0 in range(lo, hi, 2):
        c1 = min(c0 + 2, hi)
        k0 = max(c0 - p.S + 1, p.n - p.hb)
        k1 = min(c1 - 1, 2 * p.n + p.hb - 2) + 1
        value = jnp.dot(
            rows[:, (k0 + p.hb - p.n) * b : (k1 + p.hb - p.n) * b],
            dense[k0 * b : k1 * b, c0 * b : c1 * b],
            preferred_element_type=jnp.float32,
        )
        for c in range(c0, c1):
            for i in range(p.n):
                t = c - p.n - i
                finish(i, t if 0 <= t < p.S else None, c - p.n, value[i * b : (i + 1) * b, (c - c0) * b : (c - c0 + 1) * b])


def mask_of(p, marks, i, t):
    return marks[t // p.g, i * p.g + t % p.g : i * p.g + t % p.g + 1, :]


def row_blocks(ref, r, e, p):
    return ref[pl.ds((r * p.g + e) * p.b, p.b), :]


def polynomial_kernel(p, *refs):
    count = 1 + 2 * p.steps
    steps = range(1, p.steps + 1)
    first_table, last_table, first_message, last_message, beyond = refs[:5]
    refs = refs[5:]
    root = split(refs[:count], p.steps)
    inverse = split(refs[count : 2 * count], p.steps)
    poly, own_sum, across, aside, marks = refs[2 * count : 5 + 2 * count]
    dense, left, guarded = refs[5 + 2 * count :]
    b = p.b
    par, z = place_of()
    clear_outside(p, dense)
    fill(p, dense, root, steps)
    fill_own(p, dense, beyond, par * (2 * p.n), z)
    fill_halo(p, dense, first_message, first_table)
    fill_halo(p, dense, last_message, last_table)
    for i in range(p.n):
        for c in list(range(i)) + list(range(i + p.S, p.span)):
            left[at(i, b), at(c, b)] = jnp.zeros((b, b), jnp.bfloat16)

    def visit(ref, own, group):
        if own:
            for r in range(p.n):
                for e in range(p.g):
                    left[at(r, b), at(r + p.g * group + e, b)] = row_blocks(ref, r, e, p)

    each_piece(p, inverse, steps, visit)

    def note(ref, own, group):
        if own:
            marks[group] = ref[p.n * p.g * b : p.unit, :].astype(jnp.float32)

    each_piece(p, root, steps, note)
    eye = (
        lax.broadcasted_iota(jnp.int32, (b, b), 0) == lax.broadcasted_iota(jnp.int32, (b, b), 1)
    ).astype(jnp.float32)
    guarded[:, : p.n * b] = jnp.zeros((p.n * b, p.n * b), jnp.bfloat16)
    guarded[:, (p.n + p.span) * b :] = jnp.zeros((p.n * b, p.n * b), jnp.bfloat16)

    def finish(i, t, column, value):
        if t is None:
            value = jnp.zeros((b, b), jnp.bfloat16)
        else:
            value = -0.5 * (value * mask_of(p, marks, i, t))
            if t == p.hb:
                value = 1.5 * eye + value
            value = value.astype(jnp.bfloat16)
        poly[at(i, b), at(column, b)] = value
        guarded[at(i, b), at(column + p.n, b)] = value

    band_matmul(p, left, dense, finish)

    def meet(k):
        return jnp.dot(
            dense[at(k, b), (p.n + p.hb) * b : (2 * p.n + p.hb) * b],
            guarded[:, pl.ds(pl.multiple_of((k + p.g * z) * b, b), p.g * b)],
            preferred_element_type=jnp.float32,
        )

    for r in range(p.n):
        value = meet(p.n + r)
        for e in range(p.g):
            own_sum[r, e] = value[:, e * b : (e + 1) * b]
    for out, base in ((across, par * (2 * p.n)), (aside, (1 - par) * (2 * p.n))):
        for r in range(p.n):
            value = meet(base + r)
            for e in range(p.g):
                out[r, e] = value[:, e * b : (e + 1) * b].astype(jnp.bfloat16)


def polynomial(p, tables, messages, root, inverse):
    args = [root[0], *root[1], *root[2], inverse[0], *inverse[1], *inverse[2]]
    b = p.b
    part = (p.n, p.g, b, b)
    return pl.pallas_call(
        functools.partial(polynomial_kernel, p),
        out_shape=(
            jax.ShapeDtypeStruct((p.n * b, p.span * b), jnp.bfloat16),
            jax.ShapeDtypeStruct(part, jnp.float32),
            jax.ShapeDtypeStruct(part, jnp.bfloat16),
            jax.ShapeDtypeStruct(part, jnp.bfloat16),
            jax.ShapeDtypeStruct((p.G, p.mask_rows, b), jnp.float32),
        ),
        in_specs=smem(2) + vmem(3 + len(args)),
        out_specs=tuple(vmem(5)),
        scratch_shapes=[
            pltpu.VMEM((3 * p.n * b, p.width * b), jnp.bfloat16),
            pltpu.VMEM((p.n * b, p.span * b), jnp.bfloat16),
            pltpu.VMEM((p.n * b, (2 * p.n + p.span) * b), jnp.bfloat16),
        ],
        compiler_params=params(),
        name="polynomial",
    )(*tables, *messages, *args)


def row_matmul(p, rows, dense, i, z):
    b = p.b
    return jnp.dot(
        rows[i * b : (i + 1) * b, i * b : (i + p.S) * b],
        dense[(p.n + i - p.hb) * b : (p.n + i + p.hb) * b, pl.ds(pl.multiple_of((p.n + i + p.g * z) * b, b), p.g * b)],
        preferred_element_type=jnp.float32,
    )


def inverse_main_kernel(p, *refs):
    poly, refs, out, dense = refs[0], refs[1:-2], refs[-2], refs[-1]
    b = p.b
    par, _ = place_of()
    clear_outside(p, dense)
    base = par * (2 * p.n)
    for r in range(p.n):
        dense[at(base + r, b), :] = jnp.zeros((b, p.width * b), jnp.bfloat16)
    fill(p, dense, split(refs, p.steps), range(1, p.steps + 1))

    def finish(i, t, column, value):
        if t is not None:
            out[at(i, b), at(column, b)] = value

    band_matmul(p, poly, dense, finish)


def inverse_main(p, poly, inverse):
    args = [poly, inverse[0], *inverse[1], *inverse[2]]
    b = p.b
    return pl.pallas_call(
        functools.partial(inverse_main_kernel, p),
        out_shape=jax.ShapeDtypeStruct((p.n * b, p.span * b), jnp.float32),
        in_specs=vmem(len(args)),
        out_specs=vmem(1)[0],
        scratch_shapes=[pltpu.VMEM((3 * p.n * b, p.width * b), jnp.bfloat16)],
        compiler_params=params(),
        name="inverse_main",
    )(*args)


def inverse_kernel(p, table, last_table, poly, main, marks, message, last_message, inverse_out, next_rows, band):
    b = p.b
    par, z = place_of()
    band[...] = jnp.zeros_like(band)

    def place(codes, blocks):
        length = blocks.shape[0]

        @pl.loop(0, length)
        def _(m):
            code = codes[(z * 2 + par) * length + m]
            row = lax.div(code, p.S)
            k = jnp.where(par == 0, row - (p.n - p.hb), row + 1)
            column = jnp.where(par == 0, row - p.n, row + p.n - (p.span - p.S)) + lax.rem(code, p.S)

            @pl.when((code >= 0) & (k < p.hb))
            def _():
                band[at(k, b), at(column, b)] = blocks[m]

    place(table, message)
    place(last_table, last_message)
    for kind in range(2):
        first = kind * (p.span - p.hb)
        shift = kind * (p.span - p.S)

        @pl.when(par == kind)
        def _():
            for c0 in range(0, p.S, 2):
                c1 = min(c0 + 2, p.S)
                value = main[:, (shift + c0) * b : (shift + c1) * b] + jnp.dot(
                    poly[:, first * b : (first + p.hb) * b],
                    band[:, c0 * b : c1 * b],
                    preferred_element_type=jnp.float32,
                )
                for c in range(c0, c1):
                    for i in range(p.n):
                        t = c + shift - i
                        if 0 <= t < p.S:
                            block = value[i * b : (i + 1) * b, (c - c0) * b : (c - c0 + 1) * b]
                            next_rows[at(i, b), at(c + shift, b)] = (block * mask_of(p, marks, i, t)).astype(jnp.bfloat16)
            for c in range(p.span):
                if shift <= c < shift + p.S:
                    continue
                for i in range(p.n):
                    t = c - i
                    if 0 <= t < p.S:
                        block = main[at(i, b), at(c, b)]
                        next_rows[at(i, b), at(c, b)] = (block * mask_of(p, marks, i, t)).astype(jnp.bfloat16)

    for i in range(p.n):
        for e in range(p.g):
            inverse_out[i, e] = next_rows[at(i, b), at(i + p.g * z + e, b)]


def inverse_rows(p, tables, poly, main, marks, messages):
    b = p.b
    return pl.pallas_call(
        functools.partial(inverse_kernel, p),
        out_shape=(
            jax.ShapeDtypeStruct((p.n, p.g, b, b), jnp.bfloat16),
            jax.ShapeDtypeStruct((p.n * b, p.span * b), jnp.bfloat16),
        ),
        in_specs=smem(2) + vmem(5),
        out_specs=tuple(vmem(2)),
        scratch_shapes=[pltpu.VMEM((p.hb * b, p.S * b), jnp.bfloat16)],
        compiler_params=params(),
        name="inverse",
    )(*tables, poly, main, marks, *messages)


def lowdin_kernel(p, *refs):
    next_rows, own, partner, beyond = refs[:4]
    held, swapped = refs[4 : 4 + p.near], refs[4 + p.near : 4 + 2 * p.near]
    lowdin_out, band = refs[4 + 2 * p.near :]
    b = p.b
    _, z = place_of()
    clear_outside(p, band)
    fill_near(p, band, own, partner, beyond, held, swapped)
    own_marks = own[p.n * p.g * b : p.unit, :].astype(jnp.float32)
    for i in range(p.n):
        value = row_matmul(p, next_rows, band, i, z)
        for e in range(p.g):
            m = own_marks[i * p.g + e : i * p.g + e + 1, :]
            lowdin_out[i, e] = (value[:, e * b : (e + 1) * b] * m).astype(jnp.bfloat16)


def lowdin(p, next_rows, hamilton):
    b = p.b
    return pl.pallas_call(
        functools.partial(lowdin_kernel, p),
        out_shape=jax.ShapeDtypeStruct((p.n, p.g, b, b), jnp.bfloat16),
        in_specs=vmem(1 + len(hamilton)),
        out_specs=vmem(1)[0],
        scratch_shapes=[pltpu.VMEM((3 * p.n * b, p.width * b), jnp.bfloat16)],
        compiler_params=params(),
        name="lowdin",
    )(next_rows, *hamilton)


def join_kernel(p, own_ref, partner_ref, own_mask, partner_mask, out_ref, *copies):
    b = p.b
    rows = lax.broadcasted_iota(jnp.int32, (p.mask_rows, b), 0)
    for half, x_ref, mask_ref in ((0, own_ref, own_mask), (1, partner_ref, partner_mask)):
        marks = jnp.zeros((p.mask_rows, b), jnp.float32)
        for r in range(p.n):
            for e in range(p.g):
                m = (mask_ref[e, r] > 0).astype(jnp.float32)
                marks = jnp.where(rows == r * p.g + e, m, marks)
                value = (x_ref[r, e].astype(jnp.float32) * m).astype(jnp.bfloat16)
                block = pl.ds((r * p.g + e) * b, b)
                out_ref[half, block, :] = value
                if half == 0:
                    for copy in copies:
                        copy[block, :] = value
        out_ref[half, p.n * p.g * b :, :] = marks.astype(jnp.bfloat16)
        if half == 0:
            for copy in copies:
                copy[p.n * p.g * b :, :] = marks.astype(jnp.bfloat16)


def join(p, own, partner, own_mask, partner_mask, copies):
    alone = jax.ShapeDtypeStruct((p.unit, p.b), jnp.bfloat16)
    return pl.pallas_call(
        functools.partial(join_kernel, p),
        out_shape=(jax.ShapeDtypeStruct((2, p.unit, p.b), jnp.bfloat16),) + (alone,) * copies,
        in_specs=vmem(2) + smem(2),
        out_specs=tuple(vmem(1 + copies)),
        compiler_params=params(),
        name="join",
    )(own, partner, own_mask, partner_mask)


def finish_kernel(p, own_sum, across, aside, root_own, out):
    marks = root_own[0, p.n * p.g * p.b : p.unit, :].astype(jnp.float32)
    for r in range(p.n):
        for e in range(p.g):
            total = own_sum[r, e] + across[r, e].astype(jnp.float32) + aside[r, e].astype(jnp.float32)
            out[r, e] = (total * marks[r * p.g + e : r * p.g + e + 1, :]).astype(jnp.bfloat16)


def finish(p, own_sum, across, aside, root_own):
    return pl.pallas_call(
        functools.partial(finish_kernel, p),
        out_shape=jax.ShapeDtypeStruct((p.n, p.g, p.b, p.b), jnp.bfloat16),
        in_specs=vmem(4),
        out_specs=vmem(1)[0],
        compiler_params=params(),
        name="finish",
    )(own_sum, across, aside, root_own)


def body(root_margin, inverse_root, hamiltonian, margin_mask, hamilton_mask):
    rows, group, block = root_margin.shape[0], root_margin.shape[1], root_margin.shape[2]
    groups, cannon = lax.axis_size("rep"), lax.axis_size("cannon")
    p = Plan(rows, group, groups, block, cannon)

    def relay_route(step):
        route = []
        for c in range(cannon):
            for z in range(groups):
                sign = 1 - 2 * (c % 2)
                if 0 <= z - sign * (step - 1) < groups and 0 <= z + sign < groups:
                    route.append((c * groups + z, c * groups + z + sign))
        return route

    aside_route = [(c, c ^ 1) for c in range(cannon)]
    across_route = [(c, (c + 1) % cannon if c % 2 else (c - 1) % cannon) for c in range(cannon)]

    def relay(x, step):
        return lax.ppermute(x, AXES, relay_route(step))

    def aside(x):
        return lax.ppermute(x, "cannon", aside_route)

    def across(x):
        return lax.ppermute(x, "cannon", across_route)

    everything = list(range(1, p.steps + 1))
    close = everything[:-1]
    near_lists, far_lists = p.halo_split(False, None)
    inverse_near, inverse_far = p.halo_split(True, rows * group)
    own_mask = margin_mask.T
    partner_mask = aside(own_mask)
    pieces = []
    for x, copies in ((root_margin, 1), (inverse_root, 0)):
        partner = aside(x)
        both, *alone = join(p, x, partner, own_mask, partner_mask, copies)
        if copies:
            root_beyond = across(alone[0])
        held, swapped = [], []
        step = both
        for s in everything:
            step = relay(step, s)
            held.append(step)
            swapped.append(aside(step))
        pieces.append((both, held, swapped))
    root, inverse = pieces

    own = prep(p, hamiltonian, hamilton_mask)
    partner = aside(own)
    beyond = across(own)
    beside = aside(beyond)
    both = pack_near(p, own, partner, beside)
    held, swapped = [], []
    for s in range(1, p.near + 1):
        if s > 1:
            both = trim(p, both, p.near_len[s])
        both = relay(both, s)
        held.append(both)
        swapped.append(aside(both))
    hamilton = (own, partner, beyond, *held, *swapped)

    near_message = pack(p, root, close, False, near_lists)
    near_message = across(near_message)
    far_message = pack(p, root, everything, False, far_lists)
    far_message = across(far_message)
    first_message = pack(p, inverse, close, True, inverse_near)
    first_message = across(first_message)
    last_message = pack(p, inverse, everything, True, inverse_far)
    last_message = across(last_message)
    tables = (p.entries(near_lists), p.entries(far_lists))
    poly, own_sum, across_sum, aside_sum, marks = polynomial(
        p, tables, (near_message, far_message, root_beyond), root, inverse
    )
    across_sum = across(across_sum)
    aside_sum = aside(aside_sum)
    main = inverse_main(p, poly, inverse)
    inverse_next, next_rows = inverse_rows(
        p, (p.entries(inverse_near), p.entries(inverse_far)), poly, main, marks, (first_message, last_message)
    )
    lowdin_product = lowdin(p, next_rows, hamilton)
    root_next = finish(p, own_sum, across_sum, aside_sum, root[0])
    return root_next, inverse_next, lowdin_product


def solution(mesh):
    blocks = P("cannon", "rep", None, None)
    masks = P("cannon", "rep")
    return jax.shard_map(
        body,
        mesh=mesh,
        in_specs=(blocks, blocks, blocks, masks, masks),
        out_specs=(blocks, blocks, blocks),
        check_vma=False,
    )
```

```python
import functools

import jax
import jax.numpy as jnp
from jax import lax
from jax.experimental import pallas as pl
from jax.experimental.pallas import tpu as pltpu
from jax.sharding import PartitionSpec as P


VMEM_LIMIT = 22 * 1024 * 1024
AXES = ("cannon", "rep")


class Plan:
    def __init__(self, rows, group, groups, block, cannon):
        slots = group * groups
        half = slots // 2
        assert rows >= half and cannon % 2 == 0
        self.n, self.g, self.G, self.S, self.hb, self.b = rows, group, groups, slots, half, block
        self.mask_rows = -(-rows * group // 16) * 16
        self.unit = rows * group * block + self.mask_rows
        self.width = 3 * rows + slots - 1
        self.span = rows + slots - 1
        self.steps = groups - 1
        full_up, full_dn = set(), set()
        for i in range(rows):
            for t in range(slots):
                for s in range(slots):
                    u = t - s + half
                    k = i + s - half
                    if not 0 <= u < slots:
                        continue
                    if k < 0:
                        full_up.add((k + rows, u))
                    elif k >= rows:
                        full_dn.add((k - rows, u))
        for r in range(rows):
            for s in range(slots):
                if 0 <= r - rows + s - half < rows:
                    full_up.add((r, s))
                if 0 <= r + rows + s - half < rows:
                    full_dn.add((r, s))
        self.full = (sorted(full_up), sorted(full_dn))

        def needed(away):
            found = set()
            for i in range(rows):
                for e_out in range(group):
                    for e in range(group):
                        shift = group * away + e_out - e
                        if 0 <= shift + half < slots:
                            found.add((i + shift, e))
            return found

        self.near = max([d for d in range(1, groups) if needed(d) or needed(-d)], default=0)
        self.ahead, self.behind = {}, {}
        for lists, sign in ((self.ahead, 1), (self.behind, -1)):
            so_far = []
            for d in range(self.near, 0, -1):
                so_far = so_far + sorted(needed(sign * d) - set(so_far))
                lists[d] = so_far
        self.near_len = {d: max(len(self.ahead[d]), len(self.behind[d])) for d in range(1, self.near + 1)}

    def halo(self, steps):
        out = []
        for z in range(self.G):
            kinds = []
            for kind in range(2):
                kinds.append([(r, u) for r, u in self.full[kind] if abs(u // self.g - z) in steps])
            out.append(kinds)
        return out

    def halo_parts(self, stages):
        fresh = [self.halo(steps) for steps in stages]
        sizes = [self.length(lists) for lists in fresh]
        total = max(
            sum(len(lists[z][kind]) for lists in fresh) for z in range(self.G) for kind in range(2)
        )
        for m in range(len(sizes) - 1):
            sizes[m] = max(0, min(sizes[m], total - sum(sizes[m + 1 :])))
        for z in range(self.G):
            for kind in range(2):
                waiting = 0
                for m in range(len(sizes)):
                    waiting = max(0, waiting + len(fresh[m][z][kind]) - sizes[m])
                if waiting:
                    sizes[0] += waiting
        parts = []
        for z in range(self.G):
            kinds = []
            for kind in range(2):
                waiting, row = [], []
                for m, size in enumerate(sizes):
                    waiting = waiting + fresh[m][z][kind]
                    row.append(waiting[:size])
                    waiting = waiting[size:]
                assert not waiting
                kinds.append(row)
            parts.append(kinds)
        return [[[parts[z][kind][m] for kind in range(2)] for z in range(self.G)] for m in range(len(sizes))]

    def length(self, lists):
        return max(len(x) for kinds in lists for x in kinds)

    def positions(self, lists):
        length = self.length(lists)
        out = []
        for z in range(self.G):
            for kind in range(2):
                for r in range(self.n):
                    for u in range(-(self.G - 1) * self.g, (2 * self.G - 1) * self.g):
                        block = (r, u)
                        out.append(lists[z][kind].index(block) if block in lists[z][kind] else length)
        return jnp.asarray(out, jnp.int32)

    def targets(self, lists, where, spare):
        length = self.length(lists)
        out = []
        for z in range(self.G):
            for kind in range(2):
                row = [where(kind, r, u) for r, u in lists[z][kind]]
                row += [None] * (length - len(row))
                out += [spare * 64 if x is None else x[0] * 64 + x[1] for x in row]
        assert self.width < 64
        return jnp.asarray(out, jnp.int32)

    def dense_targets(self, lists):
        def where(kind, r, u):
            k = kind * 2 * self.n + r
            return k, k + u

        return self.targets(lists, where, 3 * self.n)

    def reach_targets(self, lists):
        def where(kind, r, u):
            k = kind * 2 * self.n + r
            column = k + u - (self.n + self.hb)
            return (k, column) if 0 <= column < self.n else None

        return self.targets(lists, where, 3 * self.n)

    def band_targets(self, lists):
        def where(kind, r, u):
            k = r + 1 if kind else r - (self.n - self.hb)
            column = u + (r + self.n - (self.span - self.S) if kind else r - self.n)
            return (k, column) if 0 <= k < self.hb and 0 <= column < self.S else None

        return self.targets(lists, where, self.hb)


def place_of():
    par = lax.rem(lax.axis_index("cannon"), 2)
    return par, lax.axis_index("rep")


def at(index, block):
    if isinstance(index, int):
        return pl.ds(index * block, block)
    return pl.ds(pl.multiple_of(index * block, block), block)


def prep_kernel(p, x_ref, mask_ref, out_ref, staged, done):
    b = p.b
    copy = pltpu.make_async_copy(x_ref, staged, done)
    copy.start()
    rows = lax.broadcasted_iota(jnp.int32, (p.mask_rows, b), 0)
    marks = jnp.zeros((p.mask_rows, b), jnp.float32)
    values = []
    for r in range(p.n):
        for e in range(p.g):
            m = (mask_ref[e, r] > 0).astype(jnp.float32)
            values.append(m)
            marks = jnp.where(rows == r * p.g + e, m, marks)
    out_ref[p.n * p.g * b :, :] = marks.astype(jnp.bfloat16)
    copy.wait()
    for r in range(p.n):
        for e in range(p.g):
            value = staged[r, e].astype(jnp.float32) * values[r * p.g + e]
            out_ref[pl.ds((r * p.g + e) * b, b), :] = value.astype(jnp.bfloat16)


def vmem(count):
    return [pl.BlockSpec(memory_space=pltpu.VMEM)] * count


def smem(count):
    return [pl.BlockSpec(memory_space=pltpu.SMEM)] * count


def params(limit=VMEM_LIMIT):
    return pltpu.CompilerParams(vmem_limit_bytes=limit)


def prep(p, x, mask):
    return pl.pallas_call(
        functools.partial(prep_kernel, p),
        out_shape=jax.ShapeDtypeStruct((p.unit, p.b), jnp.bfloat16),
        in_specs=[pl.BlockSpec(memory_space=pltpu.HBM)] + smem(1),
        out_specs=vmem(1)[0],
        scratch_shapes=[pltpu.VMEM((p.n, p.g, p.b, p.b), jnp.bfloat16), pltpu.SemaphoreType.DMA(())],
        compiler_params=params(),
        name="prep",
    )(x, mask.T)


def each_piece(p, pieces, steps, visit):
    par, z = place_of()
    sign = 1 - 2 * par
    own, partner, held, swapped = pieces
    if own is not None:
        visit(own, True, z)
        visit(partner, False, z)
    for m, s in enumerate(steps):
        for refs, group, order in ((held, z - sign * s, (True, False)), (swapped, z + sign * s, (False, True))):

            @pl.when((group >= 0) & (group < p.G))
            def _():
                for half in range(2):
                    visit(refs[m].at[half], order[half], group)


def split(refs, steps):
    return refs[0].at[0], refs[0].at[1], refs[1 : 1 + steps], refs[1 + steps : 1 + 2 * steps]


def pack_kernel(p, steps, with_own, *refs):
    table, refs, out, staged = refs[0], refs[1:-2], refs[-2], refs[-1]
    par, z = place_of()
    sign = 1 - 2 * par
    base = (z * 2 + (1 - par)) * (p.n * (3 * p.G - 2) * p.g)

    def take(ref, group):
        for r in range(p.n):
            for e in range(p.g):
                to = table[base + r * (3 * p.G - 2) * p.g + (group + p.G - 1) * p.g + e]
                staged[to] = row_blocks(ref, r, e, p)

    if with_own:
        take(refs[0].at[0], z)
        refs = refs[1:]
    for m, s in enumerate(steps):
        take(refs[m].at[0], z - sign * s)
        take(refs[len(steps) + m].at[1], z + sign * s)
    out[...] = staged[: out.shape[0]]


def pack(p, pieces, steps, with_own, lists):
    both, held, swapped = pieces
    args = [both] if with_own else []
    args += [held[s - 1] for s in steps] + [swapped[s - 1] for s in steps]
    length = p.length(lists)
    return pl.pallas_call(
        functools.partial(pack_kernel, p, steps, with_own),
        out_shape=jax.ShapeDtypeStruct((length, p.b, p.b), jnp.bfloat16),
        in_specs=smem(1) + vmem(len(args)),
        out_specs=vmem(1)[0],
        scratch_shapes=[pltpu.VMEM((length + 1, p.b, p.b), jnp.bfloat16)],
        compiler_params=params(),
        name="pack",
    )(p.positions(lists), *args)


def pack_near_kernel(p, own, partner, beyond, out):
    par, _ = place_of()
    for kind, blocks in ((0, p.ahead[1]), (1, p.behind[1])):

        @pl.when(par == kind)
        def _():
            for m, (k, e) in enumerate(blocks):
                inside = 0 <= k < p.n
                r = k % p.n
                at_row = pl.ds((r * p.g + e) * p.b, p.b)
                out[0, m] = (own if inside else partner)[at_row, :]
                out[1, m] = (partner if inside else beyond)[at_row, :]


def pack_near(p, own, partner, beyond):
    return pl.pallas_call(
        functools.partial(pack_near_kernel, p),
        out_shape=jax.ShapeDtypeStruct((2, p.near_len[1], p.b, p.b), jnp.bfloat16),
        in_specs=vmem(3),
        out_specs=vmem(1)[0],
        compiler_params=params(),
        name="pack_near",
    )(own, partner, beyond)


def trim_kernel(x_ref, out_ref):
    out_ref[...] = x_ref[:, : out_ref.shape[1]]


def trim(p, x, length):
    return pl.pallas_call(
        trim_kernel,
        out_shape=jax.ShapeDtypeStruct((2, length, p.b, p.b), jnp.bfloat16),
        in_specs=vmem(1),
        out_specs=vmem(1)[0],
        compiler_params=params(),
        name="trim",
    )(x)


def clear_outside(p, dense):
    lo, hi = p.n, p.n + p.span
    for k in range(3 * p.n):
        left, right = max(lo, min(hi, k)), min(hi, k + p.S)
        if left > lo:
            dense[at(k, p.b), lo * p.b : left * p.b] = jnp.zeros((p.b, (left - lo) * p.b), jnp.bfloat16)
        if right < hi:
            dense[at(k, p.b), right * p.b : hi * p.b] = jnp.zeros((p.b, (hi - right) * p.b), jnp.bfloat16)


def fill(p, dense, pieces, steps, own_only=False):
    par, _ = place_of()
    aside = p.n + p.n * (1 - 2 * par)

    def visit(ref, own, group):
        if own_only and not own:
            return
        for r in range(p.n):
            k = p.n + r if own else aside + r
            for e in range(p.g):
                dense[at(k, p.b), at(k + p.g * group + e, p.b)] = ref[pl.ds((r * p.g + e) * p.b, p.b), :]

    each_piece(p, pieces, steps, visit)


def scatter(p, dense, message, table):
    par, z = place_of()
    length = message.shape[0]
    for m in range(length):
        code = table[(z * 2 + par) * length + m]
        dense[at(lax.shift_right_logical(code, 6), p.b), at(lax.bitwise_and(code, 63), p.b)] = message[m]


def fill_own(p, dense, ref, base, group):
    for r in range(p.n):
        for e in range(p.g):
            dense[at(base + r, p.b), at(base + r + p.g * group + e, p.b)] = row_blocks(ref, r, e, p)


def fill_near(p, dense, own, partner, beyond, held, swapped):
    par, z = place_of()
    sign = 1 - 2 * par
    for ref, base in ((own, p.n), (partner, p.n + p.n * sign), (beyond, par * (2 * p.n))):
        fill_own(p, dense, ref, base, z)
    for s in range(1, p.near + 1):
        for kind, first, second in ((0, p.ahead[s], p.behind[s]), (1, p.behind[s], p.ahead[s])):
            for refs, part, blocks, group in (
                (held, 0, first, z - sign * s),
                (swapped, 1, second, z + sign * s),
            ):

                @pl.when((par == kind) & (group >= 0) & (group < p.G))
                def _():
                    for m, (k, e) in enumerate(blocks):
                        dense[at(k + p.n, p.b), at(k + p.n + p.g * group + e, p.b)] = refs[s - 1][part, m]


def band_matmul(p, rows, dense, finish):
    b = p.b
    lo, hi = p.n, p.n + p.span
    for c0 in range(lo, hi, 2):
        c1 = min(c0 + 2, hi)
        k0 = max(c0 - p.S + 1, p.n - p.hb)
        k1 = min(c1 - 1, 2 * p.n + p.hb - 2) + 1
        value = jnp.dot(
            rows[:, (k0 + p.hb - p.n) * b : (k1 + p.hb - p.n) * b],
            dense[k0 * b : k1 * b, c0 * b : c1 * b],
            preferred_element_type=jnp.float32,
        )
        for c in range(c0, c1):
            for i in range(p.n):
                t = c - p.n - i
                finish(i, t if 0 <= t < p.S else None, c - p.n, value[i * b : (i + 1) * b, (c - c0) * b : (c - c0 + 1) * b])


def mask_of(p, marks, i, t):
    return marks[t // p.g, i * p.g + t % p.g : i * p.g + t % p.g + 1, :]


def row_blocks(ref, r, e, p):
    return ref[pl.ds((r * p.g + e) * p.b, p.b), :]


def add_band(p, rows, band, main, finish):
    b = p.b
    par, _ = place_of()
    for kind in range(2):
        first = kind * (p.span - p.hb)
        shift = kind * (p.span - p.S)

        @pl.when(par == kind)
        def _():
            for c0 in range(0, p.S, 2):
                c1 = min(c0 + 2, p.S)
                value = main[:, (shift + c0) * b : (shift + c1) * b] + jnp.dot(
                    rows[:, first * b : (first + p.hb) * b],
                    band[: p.hb * b, c0 * b : c1 * b],
                    preferred_element_type=jnp.float32,
                )
                for c in range(c0, c1):
                    for i in range(p.n):
                        t = c + shift - i
                        block = value[i * b : (i + 1) * b, (c - c0) * b : (c - c0 + 1) * b]
                        finish(i, t if 0 <= t < p.S else None, c + shift, block)
            for c in range(p.span):
                if not shift <= c < shift + p.S:
                    for i in range(p.n):
                        t = c - i
                        inside = 0 <= t < p.S
                        finish(i, t if inside else None, c, main[at(i, b), at(c, b)] if inside else None)


def clear_across(p, dense):
    par, _ = place_of()
    for r in range(p.n):
        dense[at(par * (2 * p.n) + r, p.b), p.n * p.b : (p.n + p.span) * p.b] = jnp.zeros((p.b, p.span * p.b), jnp.bfloat16)


def polynomial_main_kernel(p, parts, *refs):
    count = 1 + 2 * p.steps
    steps = range(1, p.steps + 1)
    tables, messages, beyond = refs[:parts], refs[parts : 2 * parts], refs[2 * parts]
    refs = refs[2 * parts + 1 :]
    root = split(refs[:count], p.steps)
    inverse = split(refs[count : 2 * count], p.steps)
    main, left, reach, marks, dense = refs[2 * count :]
    b = p.b
    par, z = place_of()
    clear_outside(p, dense)
    clear_across(p, dense)
    fill(p, dense, root, steps)
    fill_own(p, dense, beyond, par * (2 * p.n), z)
    for table, message in zip(tables, messages):
        scatter(p, dense, message, table)
    for i in range(p.n):
        for c in list(range(i)) + list(range(i + p.S, p.span)):
            left[at(i, b), at(c, b)] = jnp.zeros((b, b), jnp.bfloat16)

    def visit(ref, own, group):
        if own:
            for r in range(p.n):
                for e in range(p.g):
                    left[at(r, b), at(r + p.g * group + e, b)] = row_blocks(ref, r, e, p)

    each_piece(p, inverse, steps, visit)

    def note(ref, own, group):
        if own:
            marks[group] = ref[p.n * p.g * b : p.unit, :].astype(jnp.float32)

    each_piece(p, root, steps, note)
    reach[...] = dense[: 3 * p.n * b, (p.n + p.hb) * b : (2 * p.n + p.hb) * b]

    def finish(i, t, column, value):
        if t is not None:
            main[at(i, b), at(column, b)] = value

    band_matmul(p, left, dense, finish)


def polynomial_main(p, tables, messages, beyond, root, inverse):
    args = [*messages, beyond, root[0], *root[1], *root[2], inverse[0], *inverse[1], *inverse[2]]
    b = p.b
    return pl.pallas_call(
        functools.partial(polynomial_main_kernel, p, len(tables)),
        out_shape=(
            jax.ShapeDtypeStruct((p.n * b, p.span * b), jnp.float32),
            jax.ShapeDtypeStruct((p.n * b, p.span * b), jnp.bfloat16),
            jax.ShapeDtypeStruct((3 * p.n * b, p.n * b), jnp.bfloat16),
            jax.ShapeDtypeStruct((p.G, p.mask_rows, b), jnp.float32),
        ),
        in_specs=smem(len(tables)) + vmem(len(args)),
        out_specs=tuple(vmem(4)),
        scratch_shapes=[pltpu.VMEM(((3 * p.n + 1) * b, p.width * b), jnp.bfloat16)],
        compiler_params=params(),
        name="polynomial_main",
    )(*tables, *args)


def polynomial_kernel(p, table, reach_table, message, main, left, early, marks, poly, own_sum, across, aside, band, reach, guarded):
    b = p.b
    par, z = place_of()
    band[: p.hb * b, :] = jnp.zeros((p.hb * b, p.S * b), jnp.bfloat16)
    scatter(p, band, message, table)
    reach[: 3 * p.n * b, :] = early[...]
    scatter(p, reach, message, reach_table)
    eye = (
        lax.broadcasted_iota(jnp.int32, (b, b), 0) == lax.broadcasted_iota(jnp.int32, (b, b), 1)
    ).astype(jnp.float32)
    guarded[:, : p.n * b] = jnp.zeros((p.n * b, p.n * b), jnp.bfloat16)
    guarded[:, (p.n + p.span) * b :] = jnp.zeros((p.n * b, p.n * b), jnp.bfloat16)

    def finish(i, t, column, value):
        if t is None:
            value = jnp.zeros((b, b), jnp.bfloat16)
        else:
            value = -0.5 * (value * mask_of(p, marks, i, t))
            if t == p.hb:
                value = 1.5 * eye + value
            value = value.astype(jnp.bfloat16)
        poly[at(i, b), at(column, b)] = value
        guarded[at(i, b), at(column + p.n, b)] = value

    add_band(p, left, band, main, finish)

    def meet(k):
        return jnp.dot(
            reach[at(k, b), :],
            guarded[:, pl.ds(pl.multiple_of((k + p.g * z) * b, b), p.g * b)],
            preferred_element_type=jnp.float32,
        )

    for r in range(p.n):
        value = meet(p.n + r)
        for e in range(p.g):
            own_sum[r, e] = value[:, e * b : (e + 1) * b]
    for out, base in ((across, par * (2 * p.n)), (aside, (1 - par) * (2 * p.n))):
        for r in range(p.n):
            value = meet(base + r)
            for e in range(p.g):
                out[r, e] = value[:, e * b : (e + 1) * b].astype(jnp.bfloat16)


def polynomial(p, tables, message, main, left, reach, marks):
    b = p.b
    part = (p.n, p.g, b, b)
    return pl.pallas_call(
        functools.partial(polynomial_kernel, p),
        out_shape=(
            jax.ShapeDtypeStruct((p.n * b, p.span * b), jnp.bfloat16),
            jax.ShapeDtypeStruct(part, jnp.float32),
            jax.ShapeDtypeStruct(part, jnp.bfloat16),
            jax.ShapeDtypeStruct(part, jnp.bfloat16),
        ),
        in_specs=smem(2) + vmem(5),
        out_specs=tuple(vmem(4)),
        scratch_shapes=[
            pltpu.VMEM(((p.hb + 1) * b, p.S * b), jnp.bfloat16),
            pltpu.VMEM(((3 * p.n + 1) * b, p.n * b), jnp.bfloat16),
            pltpu.VMEM((p.n * b, (2 * p.n + p.span) * b), jnp.bfloat16),
        ],
        compiler_params=params(),
        name="polynomial",
    )(*tables, message, main, left, reach, marks)


def row_matmul(p, rows, dense, i, z):
    b = p.b
    return jnp.dot(
        rows[i * b : (i + 1) * b, i * b : (i + p.S) * b],
        dense[(p.n + i - p.hb) * b : (p.n + i + p.hb) * b, pl.ds(pl.multiple_of((p.n + i + p.g * z) * b, b), p.g * b)],
        preferred_element_type=jnp.float32,
    )


def inverse_main_kernel(p, *refs):
    poly, refs, out, dense = refs[0], refs[1:-2], refs[-2], refs[-1]
    b = p.b
    clear_outside(p, dense)
    clear_across(p, dense)
    fill(p, dense, split(refs, p.steps), range(1, p.steps + 1))

    def finish(i, t, column, value):
        if t is not None:
            out[at(i, b), at(column, b)] = value

    band_matmul(p, poly, dense, finish)


def inverse_main(p, poly, inverse):
    args = [poly, inverse[0], *inverse[1], *inverse[2]]
    b = p.b
    return pl.pallas_call(
        functools.partial(inverse_main_kernel, p),
        out_shape=jax.ShapeDtypeStruct((p.n * b, p.span * b), jnp.float32),
        in_specs=vmem(len(args)),
        out_specs=vmem(1)[0],
        scratch_shapes=[pltpu.VMEM((3 * p.n * b, p.width * b), jnp.bfloat16)],
        compiler_params=params(),
        name="inverse_main",
    )(*args)


def inverse_kernel(p, table, last_table, poly, main, marks, message, last_message, next_rows, band):
    b = p.b
    band[: p.hb * b, :] = jnp.zeros((p.hb * b, p.S * b), jnp.bfloat16)
    scatter(p, band, message, table)
    scatter(p, band, last_message, last_table)

    def finish(i, t, column, value):
        if t is not None:
            next_rows[at(i, b), at(column, b)] = (value * mask_of(p, marks, i, t)).astype(jnp.bfloat16)

    add_band(p, poly, band, main, finish)


def inverse_rows(p, tables, poly, main, marks, messages):
    b = p.b
    return pl.pallas_call(
        functools.partial(inverse_kernel, p),
        out_shape=jax.ShapeDtypeStruct((p.n * b, p.span * b), jnp.bfloat16),
        in_specs=smem(2) + vmem(5),
        out_specs=vmem(1)[0],
        scratch_shapes=[pltpu.VMEM(((p.hb + 1) * b, p.S * b), jnp.bfloat16)],
        compiler_params=params(),
        name="inverse",
    )(*tables, poly, main, marks, *messages)


def outputs_kernel(p, *refs):
    next_rows, own_sum, across, aside, root_both, own, partner, beyond = refs[:8]
    held, swapped = refs[8 : 8 + p.near], refs[8 + p.near : 8 + 2 * p.near]
    root_out, inverse_out, lowdin_out, band = refs[8 + 2 * p.near :]
    b = p.b
    _, z = place_of()
    root_marks = root_both[0, p.n * p.g * b : p.unit, :].astype(jnp.float32)
    for r in range(p.n):
        for e in range(p.g):
            inverse_out[r, e] = next_rows[at(r, b), at(r + p.g * z + e, b)]
            total = own_sum[r, e] + across[r, e].astype(jnp.float32) + aside[r, e].astype(jnp.float32)
            root_out[r, e] = (total * root_marks[r * p.g + e : r * p.g + e + 1, :]).astype(jnp.bfloat16)
    clear_outside(p, band)
    fill_near(p, band, own, partner, beyond, held, swapped)
    own_marks = own[p.n * p.g * b : p.unit, :].astype(jnp.float32)
    for i in range(p.n):
        value = row_matmul(p, next_rows, band, i, z)
        for e in range(p.g):
            m = own_marks[i * p.g + e : i * p.g + e + 1, :]
            lowdin_out[i, e] = (value[:, e * b : (e + 1) * b] * m).astype(jnp.bfloat16)


def outputs(p, next_rows, sums, root_both, hamilton):
    b = p.b
    out = jax.ShapeDtypeStruct((p.n, p.g, b, b), jnp.bfloat16)
    return pl.pallas_call(
        functools.partial(outputs_kernel, p),
        out_shape=(out, out, out),
        in_specs=vmem(5 + len(hamilton)),
        out_specs=tuple(vmem(3)),
        scratch_shapes=[pltpu.VMEM((3 * p.n * b, p.width * b), jnp.bfloat16)],
        compiler_params=params(),
        name="outputs",
    )(next_rows, *sums, root_both, *hamilton)


def join_kernel(p, own_ref, partner_ref, own_mask, partner_mask, out_ref, *copies):
    b = p.b
    rows = lax.broadcasted_iota(jnp.int32, (p.mask_rows, b), 0)
    for half, x_ref, mask_ref in ((0, own_ref, own_mask), (1, partner_ref, partner_mask)):
        marks = jnp.zeros((p.mask_rows, b), jnp.float32)
        for r in range(p.n):
            for e in range(p.g):
                m = (mask_ref[e, r] > 0).astype(jnp.float32)
                marks = jnp.where(rows == r * p.g + e, m, marks)
                value = (x_ref[r, e].astype(jnp.float32) * m).astype(jnp.bfloat16)
                block = pl.ds((r * p.g + e) * b, b)
                out_ref[half, block, :] = value
                if half == 0:
                    for copy in copies:
                        copy[block, :] = value
        out_ref[half, p.n * p.g * b :, :] = marks.astype(jnp.bfloat16)
        if half == 0:
            for copy in copies:
                copy[p.n * p.g * b :, :] = marks.astype(jnp.bfloat16)


def join(p, own, partner, own_mask, partner_mask, copies):
    alone = jax.ShapeDtypeStruct((p.unit, p.b), jnp.bfloat16)
    return pl.pallas_call(
        functools.partial(join_kernel, p),
        out_shape=(jax.ShapeDtypeStruct((2, p.unit, p.b), jnp.bfloat16),) + (alone,) * copies,
        in_specs=vmem(2) + smem(2),
        out_specs=tuple(vmem(1 + copies)),
        compiler_params=params(),
        name="join",
    )(own, partner, own_mask, partner_mask)


def body(root_margin, inverse_root, hamiltonian, margin_mask, hamilton_mask):
    rows, group, block = root_margin.shape[0], root_margin.shape[1], root_margin.shape[2]
    groups, cannon = lax.axis_size("rep"), lax.axis_size("cannon")
    p = Plan(rows, group, groups, block, cannon)

    def relay_route(step):
        route = []
        for c in range(cannon):
            for z in range(groups):
                sign = 1 - 2 * (c % 2)
                if 0 <= z - sign * (step - 1) < groups and 0 <= z + sign < groups:
                    route.append((c * groups + z, c * groups + z + sign))
        return route

    aside_route = [(c, c ^ 1) for c in range(cannon)]
    across_route = [(c, (c + 1) % cannon if c % 2 else (c - 1) % cannon) for c in range(cannon)]

    def relay(x, step):
        return lax.ppermute(x, AXES, relay_route(step))

    def aside(x):
        return lax.ppermute(x, "cannon", aside_route)

    def across(x):
        return lax.ppermute(x, "cannon", across_route)

    everything = list(range(1, p.steps + 1))
    close = everything[:-1]
    root_parts = p.halo_parts([[s] for s in everything])
    inverse_near, inverse_far = p.halo_parts([[0, *close], everything[-1:]])
    own_mask = margin_mask.T
    partner_mask = aside(own_mask)
    pieces = []
    for x, copies in ((root_margin, 1), (inverse_root, 0)):
        partner = aside(x)
        both, *alone = join(p, x, partner, own_mask, partner_mask, copies)
        if copies:
            root_beyond = across(alone[0])
        held, swapped = [], []
        step = both
        for s in everything:
            step = relay(step, s)
            held.append(step)
            swapped.append(aside(step))
        pieces.append((both, held, swapped))
    root, inverse = pieces

    own = prep(p, hamiltonian, hamilton_mask)
    partner = aside(own)
    beyond = across(own)
    beside = aside(beyond)
    both = pack_near(p, own, partner, beside)
    held, swapped = [], []
    for s in range(1, p.near + 1):
        if s > 1:
            both = trim(p, both, p.near_len[s])
        both = relay(both, s)
        held.append(both)
        swapped.append(aside(both))
    hamilton = (own, partner, beyond, *held, *swapped)

    root_messages = []
    for s, lists in zip(everything, root_parts):
        message = pack(p, root, everything[:s], False, lists)
        root_messages.append(across(message))
    first_message = pack(p, inverse, close, True, inverse_near)
    first_message = across(first_message)
    last_message = pack(p, inverse, everything, True, inverse_far)
    last_message = across(last_message)
    tables = [p.dense_targets(lists) for lists in root_parts[:-1]]
    main, left, reach, marks = polynomial_main(
        p, tables, root_messages[:-1], root_beyond, root, inverse
    )
    poly, own_sum, across_sum, aside_sum = polynomial(
        p, (p.band_targets(root_parts[-1]), p.reach_targets(root_parts[-1])), root_messages[-1], main, left, reach, marks
    )
    across_sum = across(across_sum)
    aside_sum = aside(aside_sum)
    main = inverse_main(p, poly, inverse)
    next_rows = inverse_rows(
        p, (p.band_targets(inverse_near), p.band_targets(inverse_far)), poly, main, marks, (first_message, last_message)
    )
    results = outputs(p, next_rows, (own_sum, across_sum, aside_sum), root[0], hamilton)
    return results


def solution(mesh):
    blocks = P("cannon", "rep", None, None)
    masks = P("cannon", "rep")
    return jax.shard_map(
        body,
        mesh=mesh,
        in_specs=(blocks, blocks, blocks, masks, masks),
        out_specs=(blocks, blocks, blocks),
        check_vma=False,
    )
```

```python
import functools

import jax
import jax.numpy as jnp
from jax import lax
from jax.experimental import pallas as pl
from jax.experimental.pallas import tpu as pltpu
from jax.sharding import PartitionSpec as P


VMEM_LIMIT = 22 * 1024 * 1024
AXES = ("cannon", "rep")


class Plan:
    def __init__(self, rows, group, groups, block, cannon):
        slots = group * groups
        half = slots // 2
        assert rows >= half and cannon % 2 == 0
        self.n, self.g, self.G, self.S, self.hb, self.b = rows, group, groups, slots, half, block
        self.mask_rows = -(-rows * group // 16) * 16
        self.unit = rows * group * block + self.mask_rows
        self.width = 3 * rows + slots - 1
        self.span = rows + slots - 1
        self.steps = groups - 1
        full_up, full_dn = set(), set()
        for i in range(rows):
            for t in range(slots):
                for s in range(slots):
                    u = t - s + half
                    k = i + s - half
                    if not 0 <= u < slots:
                        continue
                    if k < 0:
                        full_up.add((k + rows, u))
                    elif k >= rows:
                        full_dn.add((k - rows, u))
        for r in range(rows):
            for s in range(slots):
                if 0 <= r - rows + s - half < rows:
                    full_up.add((r, s))
                if 0 <= r + rows + s - half < rows:
                    full_dn.add((r, s))
        self.full = (sorted(full_up), sorted(full_dn))

        def needed(away):
            found = set()
            for i in range(rows):
                for e_out in range(group):
                    for e in range(group):
                        shift = group * away + e_out - e
                        if 0 <= shift + half < slots:
                            found.add((i + shift, e))
            return found

        self.near = max([d for d in range(1, groups) if needed(d) or needed(-d)], default=0)
        self.ahead, self.behind = {}, {}
        for d in range(1, self.near + 1):
            self.ahead[d], self.behind[d] = sorted(needed(d)), sorted(needed(-d))
        self.near_len = {d: max(len(self.ahead[d]), len(self.behind[d])) for d in range(1, self.near + 1)}

    def halo(self, steps):
        out = []
        for z in range(self.G):
            kinds = []
            for kind in range(2):
                kinds.append([(r, u) for r, u in self.full[kind] if abs(u // self.g - z) in steps])
            out.append(kinds)
        return out

    def halo_parts(self, stages):
        fresh = [self.halo(steps) for steps in stages]
        sizes = [self.length(lists) for lists in fresh]
        total = max(
            sum(len(lists[z][kind]) for lists in fresh) for z in range(self.G) for kind in range(2)
        )
        for m in range(len(sizes) - 1):
            sizes[m] = max(0, min(sizes[m], total - sum(sizes[m + 1 :])))
        for z in range(self.G):
            for kind in range(2):
                waiting = 0
                for m in range(len(sizes)):
                    waiting = max(0, waiting + len(fresh[m][z][kind]) - sizes[m])
                if waiting:
                    sizes[0] += waiting
        parts = []
        for z in range(self.G):
            kinds = []
            for kind in range(2):
                waiting, row = [], []
                for m, size in enumerate(sizes):
                    waiting = waiting + fresh[m][z][kind]
                    row.append(waiting[:size])
                    waiting = waiting[size:]
                assert not waiting
                kinds.append(row)
            parts.append(kinds)
        return [[[parts[z][kind][m] for kind in range(2)] for z in range(self.G)] for m in range(len(sizes))]

    def length(self, lists):
        return max(len(x) for kinds in lists for x in kinds)

    def positions(self, lists):
        length = self.length(lists)
        out = []
        for z in range(self.G):
            for kind in range(2):
                for r in range(self.n):
                    for u in range(-(self.G - 1) * self.g, (2 * self.G - 1) * self.g):
                        block = (r, u)
                        out.append(lists[z][kind].index(block) if block in lists[z][kind] else length)
        return jnp.asarray(out, jnp.int32)

    def targets(self, lists, where, spare):
        length = self.length(lists)
        out = []
        for z in range(self.G):
            for kind in range(2):
                row = [where(kind, r, u) for r, u in lists[z][kind]]
                row += [None] * (length - len(row))
                out += [spare * 64 if x is None else x[0] * 64 + x[1] for x in row]
        assert self.width < 64
        return jnp.asarray(out, jnp.int32)

    def dense_targets(self, lists):
        def where(kind, r, u):
            k = kind * 2 * self.n + r
            return k, k + u

        return self.targets(lists, where, 3 * self.n)

    def reach_targets(self, lists):
        def where(kind, r, u):
            k = kind * 2 * self.n + r
            column = k + u - (self.n + self.hb)
            return (k, column) if 0 <= column < self.n else None

        return self.targets(lists, where, 3 * self.n)

    def band_targets(self, lists):
        def where(kind, r, u):
            k = r + 1 if kind else r - (self.n - self.hb)
            column = u + (r + self.n - (self.span - self.S) if kind else r - self.n)
            return (k, column) if 0 <= k < self.hb and 0 <= column < self.S else None

        return self.targets(lists, where, self.hb)


def place_of():
    par = lax.rem(lax.axis_index("cannon"), 2)
    return par, lax.axis_index("rep")


def at(index, block):
    if isinstance(index, int):
        return pl.ds(index * block, block)
    return pl.ds(pl.multiple_of(index * block, block), block)


def prep_kernel(p, x_ref, mask_ref, out_ref, staged, done):
    b = p.b
    copy = pltpu.make_async_copy(x_ref, staged, done)
    copy.start()
    rows = lax.broadcasted_iota(jnp.int32, (p.mask_rows, b), 0)
    marks = jnp.zeros((p.mask_rows, b), jnp.float32)
    values = []
    for r in range(p.n):
        for e in range(p.g):
            m = (mask_ref[e, r] > 0).astype(jnp.float32)
            values.append(m)
            marks = jnp.where(rows == r * p.g + e, m, marks)
    out_ref[p.n * p.g * b :, :] = marks.astype(jnp.bfloat16)
    copy.wait()
    for r in range(p.n):
        for e in range(p.g):
            value = staged[r, e].astype(jnp.float32) * values[r * p.g + e]
            out_ref[pl.ds((r * p.g + e) * b, b), :] = value.astype(jnp.bfloat16)


def vmem(count):
    return [pl.BlockSpec(memory_space=pltpu.VMEM)] * count


def smem(count):
    return [pl.BlockSpec(memory_space=pltpu.SMEM)] * count


def params(limit=VMEM_LIMIT):
    return pltpu.CompilerParams(vmem_limit_bytes=limit)


def prep(p, x, mask):
    return pl.pallas_call(
        functools.partial(prep_kernel, p),
        out_shape=jax.ShapeDtypeStruct((p.unit, p.b), jnp.bfloat16),
        in_specs=[pl.BlockSpec(memory_space=pltpu.HBM)] + smem(1),
        out_specs=vmem(1)[0],
        scratch_shapes=[pltpu.VMEM((p.n, p.g, p.b, p.b), jnp.bfloat16), pltpu.SemaphoreType.DMA(())],
        compiler_params=params(),
        name="prep",
    )(x, mask.T)


def each_piece(p, pieces, steps, visit):
    par, z = place_of()
    sign = 1 - 2 * par
    own, partner, held, swapped = pieces
    if own is not None:
        visit(own, True, z)
        visit(partner, False, z)
    for m, s in enumerate(steps):
        for refs, group, order in ((held, z - sign * s, (True, False)), (swapped, z + sign * s, (False, True))):

            @pl.when((group >= 0) & (group < p.G))
            def _():
                for half in range(2):
                    visit(refs[m].at[half], order[half], group)


def split(refs, steps):
    return refs[0].at[0], refs[0].at[1], refs[1 : 1 + steps], refs[1 + steps : 1 + 2 * steps]


def pack_kernel(p, steps, with_own, *refs):
    table, refs, out, staged = refs[0], refs[1:-2], refs[-2], refs[-1]
    par, z = place_of()
    sign = 1 - 2 * par
    base = (z * 2 + (1 - par)) * (p.n * (3 * p.G - 2) * p.g)

    def take(ref, group):
        for r in range(p.n):
            for e in range(p.g):
                to = table[base + r * (3 * p.G - 2) * p.g + (group + p.G - 1) * p.g + e]
                staged[to] = row_blocks(ref, r, e, p)

    if with_own:
        take(refs[0].at[0], z)
        refs = refs[1:]
    for m, s in enumerate(steps):
        take(refs[m].at[0], z - sign * s)
        take(refs[len(steps) + m].at[1], z + sign * s)
    out[...] = staged[: out.shape[0]]


def pack(p, pieces, steps, with_own, lists):
    both, held, swapped = pieces
    args = [both] if with_own else []
    args += [held[s - 1] for s in steps] + [swapped[s - 1] for s in steps]
    length = p.length(lists)
    return pl.pallas_call(
        functools.partial(pack_kernel, p, steps, with_own),
        out_shape=jax.ShapeDtypeStruct((length, p.b, p.b), jnp.bfloat16),
        in_specs=smem(1) + vmem(len(args)),
        out_specs=vmem(1)[0],
        scratch_shapes=[pltpu.VMEM((length + 1, p.b, p.b), jnp.bfloat16)],
        compiler_params=params(),
        name="pack",
    )(p.positions(lists), *args)


def pack_near_kernel(p, own, partner, beyond, *outs):
    par, _ = place_of()
    for kind, lists in ((0, p.ahead), (1, p.behind)):

        @pl.when(par == kind)
        def _():
            for d, out in enumerate(outs, 1):
                for m, (k, e) in enumerate(lists[d]):
                    inside = 0 <= k < p.n
                    r = k % p.n
                    at_row = pl.ds((r * p.g + e) * p.b, p.b)
                    out[0, m] = (own if inside else partner)[at_row, :]
                    out[1, m] = (partner if inside else beyond)[at_row, :]


def pack_near(p, own, partner, beyond):
    return pl.pallas_call(
        functools.partial(pack_near_kernel, p),
        out_shape=tuple(
            jax.ShapeDtypeStruct((2, p.near_len[d], p.b, p.b), jnp.bfloat16) for d in range(1, p.near + 1)
        ),
        in_specs=vmem(3),
        out_specs=tuple(vmem(p.near)),
        compiler_params=params(),
        name="pack_near",
    )(own, partner, beyond)


def clear_outside(p, dense):
    lo, hi = p.n, p.n + p.span
    for k in range(3 * p.n):
        left, right = max(lo, min(hi, k)), min(hi, k + p.S)
        if left > lo:
            dense[at(k, p.b), lo * p.b : left * p.b] = jnp.zeros((p.b, (left - lo) * p.b), jnp.bfloat16)
        if right < hi:
            dense[at(k, p.b), right * p.b : hi * p.b] = jnp.zeros((p.b, (hi - right) * p.b), jnp.bfloat16)


def fill(p, dense, pieces, steps, own_only=False):
    par, _ = place_of()
    aside = p.n + p.n * (1 - 2 * par)

    def visit(ref, own, group):
        if own_only and not own:
            return
        for r in range(p.n):
            k = p.n + r if own else aside + r
            for e in range(p.g):
                dense[at(k, p.b), at(k + p.g * group + e, p.b)] = ref[pl.ds((r * p.g + e) * p.b, p.b), :]

    each_piece(p, pieces, steps, visit)


def scatter(p, dense, message, table):
    par, z = place_of()
    length = message.shape[0]
    for m in range(length):
        code = table[(z * 2 + par) * length + m]
        dense[at(lax.shift_right_logical(code, 6), p.b), at(lax.bitwise_and(code, 63), p.b)] = message[m]


def fill_own(p, dense, ref, base, group):
    for r in range(p.n):
        for e in range(p.g):
            dense[at(base + r, p.b), at(base + r + p.g * group + e, p.b)] = row_blocks(ref, r, e, p)


def fill_near(p, dense, own, partner, beyond, held, swapped):
    par, z = place_of()
    sign = 1 - 2 * par
    for ref, base in ((own, p.n), (partner, p.n + p.n * sign), (beyond, par * (2 * p.n))):
        fill_own(p, dense, ref, base, z)
    for s in range(1, p.near + 1):
        for kind, first, second in ((0, p.ahead[s], p.behind[s]), (1, p.behind[s], p.ahead[s])):
            for refs, part, blocks, group in (
                (held, 0, first, z - sign * s),
                (swapped, 1, second, z + sign * s),
            ):

                @pl.when((par == kind) & (group >= 0) & (group < p.G))
                def _():
                    for m, (k, e) in enumerate(blocks):
                        dense[at(k + p.n, p.b), at(k + p.n + p.g * group + e, p.b)] = refs[s - 1][part, m]


def band_matmul(p, rows, dense, finish):
    b = p.b
    lo, hi = p.n, p.n + p.span
    for c0 in range(lo, hi, 2):
        c1 = min(c0 + 2, hi)
        k0 = max(c0 - p.S + 1, p.n - p.hb)
        k1 = min(c1 - 1, 2 * p.n + p.hb - 2) + 1
        value = jnp.dot(
            rows[:, (k0 + p.hb - p.n) * b : (k1 + p.hb - p.n) * b],
            dense[k0 * b : k1 * b, c0 * b : c1 * b],
            preferred_element_type=jnp.float32,
        )
        for c in range(c0, c1):
            for i in range(p.n):
                t = c - p.n - i
                finish(i, t if 0 <= t < p.S else None, c - p.n, value[i * b : (i + 1) * b, (c - c0) * b : (c - c0 + 1) * b])


def mask_of(p, marks, i, t):
    return marks[t // p.g, i * p.g + t % p.g : i * p.g + t % p.g + 1, :]


def row_blocks(ref, r, e, p):
    return ref[pl.ds((r * p.g + e) * p.b, p.b), :]


def add_band(p, rows, band, main, finish):
    b = p.b
    par, _ = place_of()
    for kind in range(2):
        first = kind * (p.span - p.hb)
        shift = kind * (p.span - p.S)

        @pl.when(par == kind)
        def _():
            for c0 in range(0, p.S, 2):
                c1 = min(c0 + 2, p.S)
                value = main[:, (shift + c0) * b : (shift + c1) * b] + jnp.dot(
                    rows[:, first * b : (first + p.hb) * b],
                    band[: p.hb * b, c0 * b : c1 * b],
                    preferred_element_type=jnp.float32,
                )
                for c in range(c0, c1):
                    for i in range(p.n):
                        t = c + shift - i
                        block = value[i * b : (i + 1) * b, (c - c0) * b : (c - c0 + 1) * b]
                        finish(i, t if 0 <= t < p.S else None, c + shift, block)
            for c in range(p.span):
                if not shift <= c < shift + p.S:
                    for i in range(p.n):
                        t = c - i
                        inside = 0 <= t < p.S
                        finish(i, t if inside else None, c, main[at(i, b), at(c, b)] if inside else None)


def clear_across(p, dense):
    par, _ = place_of()
    for r in range(p.n):
        dense[at(par * (2 * p.n) + r, p.b), p.n * p.b : (p.n + p.span) * p.b] = jnp.zeros((p.b, p.span * p.b), jnp.bfloat16)


def polynomial_main_kernel(p, parts, *refs):
    count = 1 + 2 * p.steps
    steps = range(1, p.steps + 1)
    tables, messages, beyond = refs[:parts], refs[parts : 2 * parts], refs[2 * parts]
    refs = refs[2 * parts + 1 :]
    root = split(refs[:count], p.steps)
    inverse = split(refs[count : 2 * count], p.steps)
    main, left, reach, marks, dense = refs[2 * count :]
    b = p.b
    par, z = place_of()
    clear_outside(p, dense)
    clear_across(p, dense)
    fill(p, dense, root, steps)
    fill_own(p, dense, beyond, par * (2 * p.n), z)
    for table, message in zip(tables, messages):
        scatter(p, dense, message, table)
    for i in range(p.n):
        for c in list(range(i)) + list(range(i + p.S, p.span)):
            left[at(i, b), at(c, b)] = jnp.zeros((b, b), jnp.bfloat16)

    def visit(ref, own, group):
        if own:
            for r in range(p.n):
                for e in range(p.g):
                    left[at(r, b), at(r + p.g * group + e, b)] = row_blocks(ref, r, e, p)

    each_piece(p, inverse, steps, visit)

    def note(ref, own, group):
        if own:
            marks[group] = ref[p.n * p.g * b : p.unit, :].astype(jnp.float32)

    each_piece(p, root, steps, note)
    reach[...] = dense[: 3 * p.n * b, (p.n + p.hb) * b : (2 * p.n + p.hb) * b]

    def finish(i, t, column, value):
        if t is not None:
            main[at(i, b), at(column, b)] = value

    band_matmul(p, left, dense, finish)


def polynomial_main(p, tables, messages, beyond, root, inverse):
    args = [*messages, beyond, root[0], *root[1], *root[2], inverse[0], *inverse[1], *inverse[2]]
    b = p.b
    return pl.pallas_call(
        functools.partial(polynomial_main_kernel, p, len(tables)),
        out_shape=(
            jax.ShapeDtypeStruct((p.n * b, p.span * b), jnp.float32),
            jax.ShapeDtypeStruct((p.n * b, p.span * b), jnp.bfloat16),
            jax.ShapeDtypeStruct((3 * p.n * b, p.n * b), jnp.bfloat16),
            jax.ShapeDtypeStruct((p.G, p.mask_rows, b), jnp.float32),
        ),
        in_specs=smem(len(tables)) + vmem(len(args)),
        out_specs=tuple(vmem(4)),
        scratch_shapes=[pltpu.VMEM(((3 * p.n + 1) * b, p.width * b), jnp.bfloat16)],
        compiler_params=params(),
        name="polynomial_main",
    )(*tables, *args)


def polynomial_kernel(p, table, reach_table, message, main, left, early, marks, poly, own_sum, across, aside, band, reach, guarded):
    b = p.b
    par, z = place_of()
    band[: p.hb * b, :] = jnp.zeros((p.hb * b, p.S * b), jnp.bfloat16)
    scatter(p, band, message, table)
    reach[: 3 * p.n * b, :] = early[...]
    scatter(p, reach, message, reach_table)
    eye = (
        lax.broadcasted_iota(jnp.int32, (b, b), 0) == lax.broadcasted_iota(jnp.int32, (b, b), 1)
    ).astype(jnp.float32)
    guarded[:, : p.n * b] = jnp.zeros((p.n * b, p.n * b), jnp.bfloat16)
    guarded[:, (p.n + p.span) * b :] = jnp.zeros((p.n * b, p.n * b), jnp.bfloat16)

    def finish(i, t, column, value):
        if t is None:
            value = jnp.zeros((b, b), jnp.bfloat16)
        else:
            value = -0.5 * (value * mask_of(p, marks, i, t))
            if t == p.hb:
                value = 1.5 * eye + value
            value = value.astype(jnp.bfloat16)
        poly[at(i, b), at(column, b)] = value
        guarded[at(i, b), at(column + p.n, b)] = value

    add_band(p, left, band, main, finish)

    def meet(k):
        return jnp.dot(
            reach[at(k, b), :],
            guarded[:, pl.ds(pl.multiple_of((k + p.g * z) * b, b), p.g * b)],
            preferred_element_type=jnp.float32,
        )

    for r in range(p.n):
        value = meet(p.n + r)
        for e in range(p.g):
            own_sum[r, e] = value[:, e * b : (e + 1) * b]
    for out, base in ((across, par * (2 * p.n)), (aside, (1 - par) * (2 * p.n))):
        for r in range(p.n):
            value = meet(base + r)
            for e in range(p.g):
                out[r, e] = value[:, e * b : (e + 1) * b].astype(jnp.bfloat16)


def polynomial(p, tables, message, main, left, reach, marks):
    b = p.b
    part = (p.n, p.g, b, b)
    return pl.pallas_call(
        functools.partial(polynomial_kernel, p),
        out_shape=(
            jax.ShapeDtypeStruct((p.n * b, p.span * b), jnp.bfloat16),
            jax.ShapeDtypeStruct(part, jnp.float32),
            jax.ShapeDtypeStruct(part, jnp.bfloat16),
            jax.ShapeDtypeStruct(part, jnp.bfloat16),
        ),
        in_specs=smem(2) + vmem(5),
        out_specs=tuple(vmem(4)),
        scratch_shapes=[
            pltpu.VMEM(((p.hb + 1) * b, p.S * b), jnp.bfloat16),
            pltpu.VMEM(((3 * p.n + 1) * b, p.n * b), jnp.bfloat16),
            pltpu.VMEM((p.n * b, (2 * p.n + p.span) * b), jnp.bfloat16),
        ],
        compiler_params=params(),
        name="polynomial",
    )(*tables, message, main, left, reach, marks)


def row_matmul(p, rows, dense, i, z):
    b = p.b
    return jnp.dot(
        rows[i * b : (i + 1) * b, i * b : (i + p.S) * b],
        dense[(p.n + i - p.hb) * b : (p.n + i + p.hb) * b, pl.ds(pl.multiple_of((p.n + i + p.g * z) * b, b), p.g * b)],
        preferred_element_type=jnp.float32,
    )


def inverse_main_kernel(p, *refs):
    poly, refs, out, dense = refs[0], refs[1:-2], refs[-2], refs[-1]
    b = p.b
    clear_outside(p, dense)
    clear_across(p, dense)
    fill(p, dense, split(refs, p.steps), range(1, p.steps + 1))

    def finish(i, t, column, value):
        if t is not None:
            out[at(i, b), at(column, b)] = value

    band_matmul(p, poly, dense, finish)


def inverse_main(p, poly, inverse):
    args = [poly, inverse[0], *inverse[1], *inverse[2]]
    b = p.b
    return pl.pallas_call(
        functools.partial(inverse_main_kernel, p),
        out_shape=jax.ShapeDtypeStruct((p.n * b, p.span * b), jnp.float32),
        in_specs=vmem(len(args)),
        out_specs=vmem(1)[0],
        scratch_shapes=[pltpu.VMEM((3 * p.n * b, p.width * b), jnp.bfloat16)],
        compiler_params=params(),
        name="inverse_main",
    )(*args)


def inverse_kernel(p, table, last_table, poly, main, marks, message, last_message, next_rows, band):
    b = p.b
    band[: p.hb * b, :] = jnp.zeros((p.hb * b, p.S * b), jnp.bfloat16)
    scatter(p, band, message, table)
    scatter(p, band, last_message, last_table)

    def finish(i, t, column, value):
        if t is not None:
            next_rows[at(i, b), at(column, b)] = (value * mask_of(p, marks, i, t)).astype(jnp.bfloat16)

    add_band(p, poly, band, main, finish)


def inverse_rows(p, tables, poly, main, marks, messages):
    b = p.b
    return pl.pallas_call(
        functools.partial(inverse_kernel, p),
        out_shape=jax.ShapeDtypeStruct((p.n * b, p.span * b), jnp.bfloat16),
        in_specs=smem(2) + vmem(5),
        out_specs=vmem(1)[0],
        scratch_shapes=[pltpu.VMEM(((p.hb + 1) * b, p.S * b), jnp.bfloat16)],
        compiler_params=params(),
        name="inverse",
    )(*tables, poly, main, marks, *messages)


def outputs_kernel(p, *refs):
    next_rows, own_sum, across, aside, root_both, own, partner, beyond = refs[:8]
    held, swapped = refs[8 : 8 + p.near], refs[8 + p.near : 8 + 2 * p.near]
    root_out, inverse_out, lowdin_out, band = refs[8 + 2 * p.near :]
    b = p.b
    _, z = place_of()
    root_marks = root_both[0, p.n * p.g * b : p.unit, :].astype(jnp.float32)
    for r in range(p.n):
        for e in range(p.g):
            inverse_out[r, e] = next_rows[at(r, b), at(r + p.g * z + e, b)]
            total = own_sum[r, e] + across[r, e].astype(jnp.float32) + aside[r, e].astype(jnp.float32)
            root_out[r, e] = (total * root_marks[r * p.g + e : r * p.g + e + 1, :]).astype(jnp.bfloat16)
    clear_outside(p, band)
    fill_near(p, band, own, partner, beyond, held, swapped)
    own_marks = own[p.n * p.g * b : p.unit, :].astype(jnp.float32)
    for i in range(p.n):
        value = row_matmul(p, next_rows, band, i, z)
        for e in range(p.g):
            m = own_marks[i * p.g + e : i * p.g + e + 1, :]
            lowdin_out[i, e] = (value[:, e * b : (e + 1) * b] * m).astype(jnp.bfloat16)


def outputs(p, next_rows, sums, root_both, hamilton):
    b = p.b
    out = jax.ShapeDtypeStruct((p.n, p.g, b, b), jnp.bfloat16)
    return pl.pallas_call(
        functools.partial(outputs_kernel, p),
        out_shape=(out, out, out),
        in_specs=vmem(5 + len(hamilton)),
        out_specs=tuple(vmem(3)),
        scratch_shapes=[pltpu.VMEM((3 * p.n * b, p.width * b), jnp.bfloat16)],
        compiler_params=params(),
        name="outputs",
    )(next_rows, *sums, root_both, *hamilton)


def join_kernel(p, ready, own_ref, partner_ref, *refs):
    b = p.b
    rows = lax.broadcasted_iota(jnp.int32, (p.mask_rows, b), 0)
    if ready:
        partner_mask, out_ref = refs
        out_ref[0] = own_ref[...]
        parts = ((1, partner_ref, partner_mask),)
    else:
        own_mask, partner_mask, out_ref = refs
        parts = ((0, own_ref, own_mask), (1, partner_ref, partner_mask))
    for half, x_ref, mask_ref in parts:
        marks = jnp.zeros((p.mask_rows, b), jnp.float32)
        for r in range(p.n):
            for e in range(p.g):
                m = (mask_ref[e, r] > 0).astype(jnp.float32)
                marks = jnp.where(rows == r * p.g + e, m, marks)
                value = (x_ref[r, e].astype(jnp.float32) * m).astype(jnp.bfloat16)
                block = pl.ds((r * p.g + e) * b, b)
                out_ref[half, block, :] = value
        out_ref[half, p.n * p.g * b :, :] = marks.astype(jnp.bfloat16)


def join(p, own, partner, own_mask, partner_mask):
    ready = own_mask is None
    masks = (partner_mask,) if ready else (own_mask, partner_mask)
    return pl.pallas_call(
        functools.partial(join_kernel, p, ready),
        out_shape=jax.ShapeDtypeStruct((2, p.unit, p.b), jnp.bfloat16),
        in_specs=vmem(2) + smem(len(masks)),
        out_specs=vmem(1)[0],
        compiler_params=params(),
        name="join",
    )(own, partner, *masks)


def body(root_margin, inverse_root, hamiltonian, margin_mask, hamilton_mask):
    rows, group, block = root_margin.shape[0], root_margin.shape[1], root_margin.shape[2]
    groups, cannon = lax.axis_size("rep"), lax.axis_size("cannon")
    p = Plan(rows, group, groups, block, cannon)

    def relay_route(step):
        route = []
        for c in range(cannon):
            for z in range(groups):
                sign = 1 - 2 * (c % 2)
                if 0 <= z - sign * (step - 1) < groups and 0 <= z + sign < groups:
                    route.append((c * groups + z, c * groups + z + sign))
        return route

    def direct_route(distance):
        route = []
        for c in range(cannon):
            for z in range(groups):
                to = z + distance * (1 - 2 * (c % 2))
                if 0 <= to < groups:
                    route.append((c * groups + z, c * groups + to))
        return route

    aside_route = [(c, c ^ 1) for c in range(cannon)]
    across_route = [(c, (c + 1) % cannon if c % 2 else (c - 1) % cannon) for c in range(cannon)]

    def relay(x, step):
        return lax.ppermute(x, AXES, relay_route(step))

    def aside(x):
        return lax.ppermute(x, "cannon", aside_route)

    def across(x):
        return lax.ppermute(x, "cannon", across_route)

    everything = list(range(1, p.steps + 1))
    close = everything[:-1]
    root_parts = p.halo_parts([[s] for s in everything])
    inverse_near, inverse_far = p.halo_parts([[0, *close], everything[-1:]])
    own_mask = margin_mask.T
    partner_mask = aside(own_mask)
    pieces = []
    alone = prep(p, root_margin, margin_mask)
    root_beyond = across(alone)
    for name, x in (("r", root_margin), ("i", inverse_root)):
        partner = aside(x)
        if name == "r":
            both = join(p, alone, partner, None, partner_mask)
        else:
            both = join(p, x, partner, own_mask, partner_mask)
        held, swapped = [], []
        step = both
        for s in everything:
            step = relay(step, s)
            held.append(step)
            swapped.append(aside(step))
        pieces.append((both, held, swapped))
    root, inverse = pieces

    own = prep(p, hamiltonian, hamilton_mask)
    partner = aside(own)
    beyond = across(own)
    beside = aside(beyond)
    near = pack_near(p, own, partner, beside)
    held, swapped = [], []
    for s, message in enumerate(near, 1):
        held.append(lax.ppermute(message, AXES, direct_route(s)))
        swapped.append(aside(held[-1]))
    hamilton = (own, partner, beyond, *held, *swapped)

    root_messages = []
    for s, lists in zip(everything, root_parts):
        message = pack(p, root, everything[:s], False, lists)
        root_messages.append(across(message))
    first_message = pack(p, inverse, close, True, inverse_near)
    first_message = across(first_message)
    last_message = pack(p, inverse, everything, True, inverse_far)
    last_message = across(last_message)
    tables = [p.dense_targets(lists) for lists in root_parts[:-1]]
    main, left, reach, marks = polynomial_main(
        p, tables, root_messages[:-1], root_beyond, root, inverse
    )
    poly, own_sum, across_sum, aside_sum = polynomial(
        p, (p.band_targets(root_parts[-1]), p.reach_targets(root_parts[-1])), root_messages[-1], main, left, reach, marks
    )
    across_sum = across(across_sum)
    aside_sum = aside(aside_sum)
    main = inverse_main(p, poly, inverse)
    next_rows = inverse_rows(
        p, (p.band_targets(inverse_near), p.band_targets(inverse_far)), poly, main, marks, (first_message, last_message)
    )
    results = outputs(p, next_rows, (own_sum, across_sum, aside_sum), root[0], hamilton)
    return results


def solution(mesh):
    blocks = P("cannon", "rep", None, None)
    masks = P("cannon", "rep")
    return jax.shard_map(
        body,
        mesh=mesh,
        in_specs=(blocks, blocks, blocks, masks, masks),
        out_specs=(blocks, blocks, blocks),
        check_vma=False,
    )
```

```python
import functools

import jax
import jax.numpy as jnp
from jax import lax
from jax.experimental import pallas as pl
from jax.experimental.pallas import tpu as pltpu
from jax.sharding import PartitionSpec as P


VMEM_LIMIT = 22 * 1024 * 1024
AXES = ("cannon", "rep")


class Plan:
    def __init__(self, rows, group, groups, block, cannon):
        slots = group * groups
        half = slots // 2
        assert rows >= half and cannon % 2 == 0
        self.n, self.g, self.G, self.S, self.hb, self.b = rows, group, groups, slots, half, block
        self.mask_rows = -(-rows * group // 16) * 16
        self.unit = rows * group * block + self.mask_rows
        self.width = 3 * rows + slots - 1
        self.span = rows + slots - 1
        self.steps = groups - 1
        full_up, full_dn = set(), set()
        for i in range(rows):
            for t in range(slots):
                for s in range(slots):
                    u = t - s + half
                    k = i + s - half
                    if not 0 <= u < slots:
                        continue
                    if k < 0:
                        full_up.add((k + rows, u))
                    elif k >= rows:
                        full_dn.add((k - rows, u))
        for r in range(rows):
            for s in range(slots):
                if 0 <= r - rows + s - half < rows:
                    full_up.add((r, s))
                if 0 <= r + rows + s - half < rows:
                    full_dn.add((r, s))
        self.full = (sorted(full_up), sorted(full_dn))

        def needed(away):
            found = set()
            for i in range(rows):
                for e_out in range(group):
                    for e in range(group):
                        shift = group * away + e_out - e
                        if 0 <= shift + half < slots:
                            found.add((i + shift, e))
            return found

        self.near = max([d for d in range(1, groups) if needed(d) or needed(-d)], default=0)
        self.ahead, self.behind = {}, {}
        for d in range(1, self.near + 1):
            self.ahead[d], self.behind[d] = sorted(needed(d)), sorted(needed(-d))
        self.near_len = {d: max(len(self.ahead[d]), len(self.behind[d])) for d in range(1, self.near + 1)}

    def halo(self, steps):
        out = []
        for z in range(self.G):
            kinds = []
            for kind in range(2):
                kinds.append([(r, u) for r, u in self.full[kind] if abs(u // self.g - z) in steps])
            out.append(kinds)
        return out

    def halo_parts(self, stages):
        fresh = [self.halo(steps) for steps in stages]
        sizes = [self.length(lists) for lists in fresh]
        total = max(
            sum(len(lists[z][kind]) for lists in fresh) for z in range(self.G) for kind in range(2)
        )
        for m in range(len(sizes) - 1):
            sizes[m] = max(0, min(sizes[m], total - sum(sizes[m + 1 :])))
        for z in range(self.G):
            for kind in range(2):
                waiting = 0
                for m in range(len(sizes)):
                    waiting = max(0, waiting + len(fresh[m][z][kind]) - sizes[m])
                if waiting:
                    sizes[0] += waiting
        parts = []
        for z in range(self.G):
            kinds = []
            for kind in range(2):
                waiting, row = [], []
                for m, size in enumerate(sizes):
                    waiting = waiting + fresh[m][z][kind]
                    row.append(waiting[:size])
                    waiting = waiting[size:]
                assert not waiting
                kinds.append(row)
            parts.append(kinds)
        return [[[parts[z][kind][m] for kind in range(2)] for z in range(self.G)] for m in range(len(sizes))]

    def length(self, lists):
        return max(len(x) for kinds in lists for x in kinds)

    def positions(self, lists):
        length = self.length(lists)
        out = []
        for z in range(self.G):
            for kind in range(2):
                for r in range(self.n):
                    for u in range(-(self.G - 1) * self.g, (2 * self.G - 1) * self.g):
                        block = (r, u)
                        out.append(lists[z][kind].index(block) if block in lists[z][kind] else length)
        return jnp.asarray(out, jnp.int32)

    def targets(self, lists, where, spare):
        length = self.length(lists)
        out = []
        for z in range(self.G):
            for kind in range(2):
                row = [where(kind, r, u) for r, u in lists[z][kind]]
                row += [None] * (length - len(row))
                out += [spare * 64 if x is None else x[0] * 64 + x[1] for x in row]
        assert self.width < 64
        return jnp.asarray(out, jnp.int32)

    def dense_targets(self, lists):
        def where(kind, r, u):
            k = kind * 2 * self.n + r
            return k, k + u

        return self.targets(lists, where, 3 * self.n)

    def reach_targets(self, lists):
        def where(kind, r, u):
            k = kind * 2 * self.n + r
            column = k + u - (self.n + self.hb)
            return (k, column) if 0 <= column < self.n else None

        return self.targets(lists, where, 3 * self.n)

    def band_targets(self, lists):
        def where(kind, r, u):
            k = r + 1 if kind else r - (self.n - self.hb)
            column = u + (r + self.n - (self.span - self.S) if kind else r - self.n)
            return (k, column) if 0 <= k < self.hb and 0 <= column < self.S else None

        return self.targets(lists, where, self.hb)


def place_of():
    par = lax.rem(lax.axis_index("cannon"), 2)
    return par, lax.axis_index("rep")


def at(index, block):
    if isinstance(index, int):
        return pl.ds(index * block, block)
    return pl.ds(pl.multiple_of(index * block, block), block)


def prep_kernel(p, x_ref, mask_ref, out_ref, staged, done):
    b = p.b
    copy = pltpu.make_async_copy(x_ref, staged, done)
    copy.start()
    rows = lax.broadcasted_iota(jnp.int32, (p.mask_rows, b), 0)
    marks = jnp.zeros((p.mask_rows, b), jnp.float32)
    values = []
    for r in range(p.n):
        for e in range(p.g):
            m = (mask_ref[e, r] > 0).astype(jnp.float32)
            values.append(m)
            marks = jnp.where(rows == r * p.g + e, m, marks)
    out_ref[p.n * p.g * b :, :] = marks.astype(jnp.bfloat16)
    copy.wait()
    for r in range(p.n):
        for e in range(p.g):
            value = staged[r, e].astype(jnp.float32) * values[r * p.g + e]
            out_ref[pl.ds((r * p.g + e) * b, b), :] = value.astype(jnp.bfloat16)


def vmem(count):
    return [pl.BlockSpec(memory_space=pltpu.VMEM)] * count


def smem(count):
    return [pl.BlockSpec(memory_space=pltpu.SMEM)] * count


def params(limit=VMEM_LIMIT):
    return pltpu.CompilerParams(vmem_limit_bytes=limit)


def prep(p, x, mask):
    return pl.pallas_call(
        functools.partial(prep_kernel, p),
        out_shape=jax.ShapeDtypeStruct((p.unit, p.b), jnp.bfloat16),
        in_specs=[pl.BlockSpec(memory_space=pltpu.HBM)] + smem(1),
        out_specs=vmem(1)[0],
        scratch_shapes=[pltpu.VMEM((p.n, p.g, p.b, p.b), jnp.bfloat16), pltpu.SemaphoreType.DMA(())],
        compiler_params=params(),
        name="prep",
    )(x, mask.T)


def each_piece(p, pieces, steps, visit):
    par, z = place_of()
    sign = 1 - 2 * par
    own, partner, held, swapped = pieces
    if own is not None:
        visit(own, True, z)
        visit(partner, False, z)
    for m, s in enumerate(steps):
        for refs, group, order in ((held, z - sign * s, (True, False)), (swapped, z + sign * s, (False, True))):

            @pl.when((group >= 0) & (group < p.G))
            def _():
                for half in range(2):
                    visit(refs[m].at[half], order[half], group)


def split(refs, steps):
    return refs[0].at[0], refs[0].at[1], refs[1 : 1 + steps], refs[1 + steps : 1 + 2 * steps]


def pack_kernel(p, steps, with_own, *refs):
    table, refs, out, staged = refs[0], refs[1:-2], refs[-2], refs[-1]
    par, z = place_of()
    sign = 1 - 2 * par
    base = (z * 2 + (1 - par)) * (p.n * (3 * p.G - 2) * p.g)

    def take(ref, group):
        for r in range(p.n):
            for e in range(p.g):
                to = table[base + r * (3 * p.G - 2) * p.g + (group + p.G - 1) * p.g + e]
                staged[to] = row_blocks(ref, r, e, p)

    if with_own:
        take(refs[0].at[0], z)
        refs = refs[1:]
    for m, s in enumerate(steps):
        take(refs[m].at[0], z - sign * s)
        take(refs[len(steps) + m].at[1], z + sign * s)
    out[...] = staged[: out.shape[0]]


def pack(p, pieces, steps, with_own, lists):
    both, held, swapped = pieces
    args = [both] if with_own else []
    args += [held[s - 1] for s in steps] + [swapped[s - 1] for s in steps]
    length = p.length(lists)
    return pl.pallas_call(
        functools.partial(pack_kernel, p, steps, with_own),
        out_shape=jax.ShapeDtypeStruct((length, p.b, p.b), jnp.bfloat16),
        in_specs=smem(1) + vmem(len(args)),
        out_specs=vmem(1)[0],
        scratch_shapes=[pltpu.VMEM((length + 1, p.b, p.b), jnp.bfloat16)],
        compiler_params=params(),
        name="pack",
    )(p.positions(lists), *args)


def pack_near_kernel(p, own, partner, beyond, *outs):
    par, _ = place_of()
    for kind, lists in ((0, p.ahead), (1, p.behind)):

        @pl.when(par == kind)
        def _():
            for d, out in enumerate(outs, 1):
                for m, (k, e) in enumerate(lists[d]):
                    inside = 0 <= k < p.n
                    r = k % p.n
                    at_row = pl.ds((r * p.g + e) * p.b, p.b)
                    out[0, m] = (own if inside else partner)[at_row, :]
                    out[1, m] = (partner if inside else beyond)[at_row, :]


def pack_near(p, own, partner, beyond):
    return pl.pallas_call(
        functools.partial(pack_near_kernel, p),
        out_shape=tuple(
            jax.ShapeDtypeStruct((2, p.near_len[d], p.b, p.b), jnp.bfloat16) for d in range(1, p.near + 1)
        ),
        in_specs=vmem(3),
        out_specs=tuple(vmem(p.near)),
        compiler_params=params(),
        name="pack_near",
    )(own, partner, beyond)


def clear_outside(p, dense):
    lo, hi = p.n, p.n + p.span
    for k in range(3 * p.n):
        left, right = max(lo, min(hi, k)), min(hi, k + p.S)
        if left > lo:
            dense[at(k, p.b), lo * p.b : left * p.b] = jnp.zeros((p.b, (left - lo) * p.b), jnp.bfloat16)
        if right < hi:
            dense[at(k, p.b), right * p.b : hi * p.b] = jnp.zeros((p.b, (hi - right) * p.b), jnp.bfloat16)


def fill(p, dense, pieces, steps, own_only=False):
    par, _ = place_of()
    aside = p.n + p.n * (1 - 2 * par)

    def visit(ref, own, group):
        if own_only and not own:
            return
        for r in range(p.n):
            k = p.n + r if own else aside + r
            for e in range(p.g):
                dense[at(k, p.b), at(k + p.g * group + e, p.b)] = ref[pl.ds((r * p.g + e) * p.b, p.b), :]

    each_piece(p, pieces, steps, visit)


def scatter(p, dense, message, table):
    par, z = place_of()
    length = message.shape[0]
    for m in range(length):
        code = table[(z * 2 + par) * length + m]
        dense[at(lax.shift_right_logical(code, 6), p.b), at(lax.bitwise_and(code, 63), p.b)] = message[m]


def fill_own(p, dense, ref, base, group):
    for r in range(p.n):
        for e in range(p.g):
            dense[at(base + r, p.b), at(base + r + p.g * group + e, p.b)] = row_blocks(ref, r, e, p)


def fill_near(p, dense, own, partner, beyond, held, swapped):
    par, z = place_of()
    sign = 1 - 2 * par
    for ref, base in ((own, p.n), (partner, p.n + p.n * sign), (beyond, par * (2 * p.n))):
        fill_own(p, dense, ref, base, z)
    for s in range(1, p.near + 1):
        for kind, first, second in ((0, p.ahead[s], p.behind[s]), (1, p.behind[s], p.ahead[s])):
            for refs, part, blocks, group in (
                (held, 0, first, z - sign * s),
                (swapped, 1, second, z + sign * s),
            ):

                @pl.when((par == kind) & (group >= 0) & (group < p.G))
                def _():
                    for m, (k, e) in enumerate(blocks):
                        dense[at(k + p.n, p.b), at(k + p.n + p.g * group + e, p.b)] = refs[s - 1][part, m]


def band_matmul(p, rows, dense, finish):
    b = p.b
    lo, hi = p.n, p.n + p.span
    for c0 in range(lo, hi, 2):
        c1 = min(c0 + 2, hi)
        k0 = max(c0 - p.S + 1, p.n - p.hb)
        k1 = min(c1 - 1, 2 * p.n + p.hb - 2) + 1
        value = jnp.dot(
            rows[:, (k0 + p.hb - p.n) * b : (k1 + p.hb - p.n) * b],
            dense[k0 * b : k1 * b, c0 * b : c1 * b],
            preferred_element_type=jnp.float32,
        )
        for c in range(c0, c1):
            for i in range(p.n):
                t = c - p.n - i
                finish(i, t if 0 <= t < p.S else None, c - p.n, value[i * b : (i + 1) * b, (c - c0) * b : (c - c0 + 1) * b])


def mask_of(p, marks, i, t):
    return marks[t // p.g, i * p.g + t % p.g : i * p.g + t % p.g + 1, :]


def row_blocks(ref, r, e, p):
    return ref[pl.ds((r * p.g + e) * p.b, p.b), :]


def add_band(p, rows, band, main, finish):
    b = p.b
    par, _ = place_of()
    for kind in range(2):
        first = kind * (p.span - p.hb)
        shift = kind * (p.span - p.S)

        @pl.when(par == kind)
        def _():
            for c0 in range(0, p.S, 2):
                c1 = min(c0 + 2, p.S)
                value = main[:, (shift + c0) * b : (shift + c1) * b] + jnp.dot(
                    rows[:, first * b : (first + p.hb) * b],
                    band[: p.hb * b, c0 * b : c1 * b],
                    preferred_element_type=jnp.float32,
                )
                for c in range(c0, c1):
                    for i in range(p.n):
                        t = c + shift - i
                        block = value[i * b : (i + 1) * b, (c - c0) * b : (c - c0 + 1) * b]
                        finish(i, t if 0 <= t < p.S else None, c + shift, block)
            for c in range(p.span):
                if not shift <= c < shift + p.S:
                    for i in range(p.n):
                        t = c - i
                        inside = 0 <= t < p.S
                        finish(i, t if inside else None, c, main[at(i, b), at(c, b)] if inside else None)


def clear_across(p, dense):
    par, _ = place_of()
    for r in range(p.n):
        dense[at(par * (2 * p.n) + r, p.b), p.n * p.b : (p.n + p.span) * p.b] = jnp.zeros((p.b, p.span * p.b), jnp.bfloat16)


def polynomial_main_kernel(p, parts, *refs):
    count = 1 + 2 * p.steps
    steps = range(1, p.steps + 1)
    tables, messages, beyond = refs[:parts], refs[parts : 2 * parts], refs[2 * parts]
    refs = refs[2 * parts + 1 :]
    root = split(refs[:count], p.steps)
    inverse = split(refs[count : 2 * count], p.steps)
    main, left, reach, marks, dense = refs[2 * count :]
    b = p.b
    par, z = place_of()
    clear_outside(p, dense)
    clear_across(p, dense)
    fill(p, dense, root, steps)
    fill_own(p, dense, beyond, par * (2 * p.n), z)
    for table, message in zip(tables, messages):
        scatter(p, dense, message, table)
    for i in range(p.n):
        for c in list(range(i)) + list(range(i + p.S, p.span)):
            left[at(i, b), at(c, b)] = jnp.zeros((b, b), jnp.bfloat16)

    def visit(ref, own, group):
        if own:
            for r in range(p.n):
                for e in range(p.g):
                    left[at(r, b), at(r + p.g * group + e, b)] = row_blocks(ref, r, e, p)

    each_piece(p, inverse, steps, visit)

    def note(ref, own, group):
        if own:
            marks[group] = ref[p.n * p.g * b : p.unit, :].astype(jnp.float32)

    each_piece(p, root, steps, note)
    reach[...] = dense[: 3 * p.n * b, (p.n + p.hb) * b : (2 * p.n + p.hb) * b]

    def finish(i, t, column, value):
        if t is not None:
            main[at(i, b), at(column, b)] = value

    band_matmul(p, left, dense, finish)


def polynomial_main(p, tables, messages, beyond, root, inverse):
    args = [*messages, beyond, root[0], *root[1], *root[2], inverse[0], *inverse[1], *inverse[2]]
    b = p.b
    return pl.pallas_call(
        functools.partial(polynomial_main_kernel, p, len(tables)),
        out_shape=(
            jax.ShapeDtypeStruct((p.n * b, p.span * b), jnp.float32),
            jax.ShapeDtypeStruct((p.n * b, p.span * b), jnp.bfloat16),
            jax.ShapeDtypeStruct((3 * p.n * b, p.n * b), jnp.bfloat16),
            jax.ShapeDtypeStruct((p.G, p.mask_rows, b), jnp.float32),
        ),
        in_specs=smem(len(tables)) + vmem(len(args)),
        out_specs=tuple(vmem(4)),
        scratch_shapes=[pltpu.VMEM(((3 * p.n + 1) * b, p.width * b), jnp.bfloat16)],
        compiler_params=params(),
        name="polynomial_main",
    )(*tables, *args)


def polynomial_kernel(p, table, reach_table, message, main, left, early, marks, poly, own_sum, across, aside, band, reach, guarded):
    b = p.b
    par, z = place_of()
    band[: p.hb * b, :] = jnp.zeros((p.hb * b, p.S * b), jnp.bfloat16)
    scatter(p, band, message, table)
    reach[: 3 * p.n * b, :] = early[...]
    scatter(p, reach, message, reach_table)
    eye = (
        lax.broadcasted_iota(jnp.int32, (b, b), 0) == lax.broadcasted_iota(jnp.int32, (b, b), 1)
    ).astype(jnp.float32)
    guarded[:, : p.n * b] = jnp.zeros((p.n * b, p.n * b), jnp.bfloat16)
    guarded[:, (p.n + p.span) * b :] = jnp.zeros((p.n * b, p.n * b), jnp.bfloat16)

    def finish(i, t, column, value):
        if t is None:
            value = jnp.zeros((b, b), jnp.bfloat16)
        else:
            value = -0.5 * (value * mask_of(p, marks, i, t))
            if t == p.hb:
                value = 1.5 * eye + value
            value = value.astype(jnp.bfloat16)
        poly[at(i, b), at(column, b)] = value
        guarded[at(i, b), at(column + p.n, b)] = value

    add_band(p, left, band, main, finish)

    def meet(k):
        return jnp.dot(
            reach[at(k, b), :],
            guarded[:, pl.ds(pl.multiple_of((k + p.g * z) * b, b), p.g * b)],
            preferred_element_type=jnp.float32,
        )

    for r in range(p.n):
        value = meet(p.n + r)
        for e in range(p.g):
            own_sum[r, e] = value[:, e * b : (e + 1) * b]
    for out, base in ((across, par * (2 * p.n)), (aside, (1 - par) * (2 * p.n))):
        for r in range(p.n):
            value = meet(base + r)
            for e in range(p.g):
                out[r, e] = value[:, e * b : (e + 1) * b].astype(jnp.bfloat16)


def polynomial(p, tables, message, main, left, reach, marks):
    b = p.b
    part = (p.n, p.g, b, b)
    return pl.pallas_call(
        functools.partial(polynomial_kernel, p),
        out_shape=(
            jax.ShapeDtypeStruct((p.n * b, p.span * b), jnp.bfloat16),
            jax.ShapeDtypeStruct(part, jnp.float32),
            jax.ShapeDtypeStruct(part, jnp.bfloat16),
            jax.ShapeDtypeStruct(part, jnp.bfloat16),
        ),
        in_specs=smem(2) + vmem(5),
        out_specs=tuple(vmem(4)),
        scratch_shapes=[
            pltpu.VMEM(((p.hb + 1) * b, p.S * b), jnp.bfloat16),
            pltpu.VMEM(((3 * p.n + 1) * b, p.n * b), jnp.bfloat16),
            pltpu.VMEM((p.n * b, (2 * p.n + p.span) * b), jnp.bfloat16),
        ],
        compiler_params=params(),
        name="polynomial",
    )(*tables, message, main, left, reach, marks)


def row_matmul(p, rows, dense, i, z):
    b = p.b
    return jnp.dot(
        rows[i * b : (i + 1) * b, i * b : (i + p.S) * b],
        dense[(p.n + i - p.hb) * b : (p.n + i + p.hb) * b, pl.ds(pl.multiple_of((p.n + i + p.g * z) * b, b), p.g * b)],
        preferred_element_type=jnp.float32,
    )


def inverse_main_kernel(p, *refs):
    poly, refs, out, dense = refs[0], refs[1:-2], refs[-2], refs[-1]
    b = p.b
    clear_outside(p, dense)
    clear_across(p, dense)
    fill(p, dense, split(refs, p.steps), range(1, p.steps + 1))

    def finish(i, t, column, value):
        if t is not None:
            out[at(i, b), at(column, b)] = value

    band_matmul(p, poly, dense, finish)


def inverse_main(p, poly, inverse):
    args = [poly, inverse[0], *inverse[1], *inverse[2]]
    b = p.b
    return pl.pallas_call(
        functools.partial(inverse_main_kernel, p),
        out_shape=jax.ShapeDtypeStruct((p.n * b, p.span * b), jnp.float32),
        in_specs=vmem(len(args)),
        out_specs=vmem(1)[0],
        scratch_shapes=[pltpu.VMEM((3 * p.n * b, p.width * b), jnp.bfloat16)],
        compiler_params=params(),
        name="inverse_main",
    )(*args)


def inverse_kernel(p, parts, *refs):
    tables, (poly, main, marks), messages = refs[:parts], refs[parts : parts + 3], refs[parts + 3 : 2 * parts + 3]
    next_rows, band = refs[2 * parts + 3 :]
    b = p.b
    band[: p.hb * b, :] = jnp.zeros((p.hb * b, p.S * b), jnp.bfloat16)
    for table, message in zip(tables, messages):
        scatter(p, band, message, table)

    def finish(i, t, column, value):
        if t is not None:
            next_rows[at(i, b), at(column, b)] = (value * mask_of(p, marks, i, t)).astype(jnp.bfloat16)

    add_band(p, poly, band, main, finish)


def inverse_rows(p, tables, poly, main, marks, messages):
    b = p.b
    return pl.pallas_call(
        functools.partial(inverse_kernel, p, len(tables)),
        out_shape=jax.ShapeDtypeStruct((p.n * b, p.span * b), jnp.bfloat16),
        in_specs=smem(len(tables)) + vmem(3 + len(tables)),
        out_specs=vmem(1)[0],
        scratch_shapes=[pltpu.VMEM(((p.hb + 1) * b, p.S * b), jnp.bfloat16)],
        compiler_params=params(),
        name="inverse",
    )(*tables, poly, main, marks, *messages)


def outputs_kernel(p, *refs):
    next_rows, own_sum, across, aside, root_both, own, partner, beyond = refs[:8]
    held, swapped = refs[8 : 8 + p.near], refs[8 + p.near : 8 + 2 * p.near]
    root_out, inverse_out, lowdin_out, band = refs[8 + 2 * p.near :]
    b = p.b
    _, z = place_of()
    root_marks = root_both[0, p.n * p.g * b : p.unit, :].astype(jnp.float32)
    for r in range(p.n):
        for e in range(p.g):
            inverse_out[r, e] = next_rows[at(r, b), at(r + p.g * z + e, b)]
            total = own_sum[r, e] + across[r, e].astype(jnp.float32) + aside[r, e].astype(jnp.float32)
            root_out[r, e] = (total * root_marks[r * p.g + e : r * p.g + e + 1, :]).astype(jnp.bfloat16)
    clear_outside(p, band)
    fill_near(p, band, own, partner, beyond, held, swapped)
    own_marks = own[p.n * p.g * b : p.unit, :].astype(jnp.float32)
    for i in range(p.n):
        value = row_matmul(p, next_rows, band, i, z)
        for e in range(p.g):
            m = own_marks[i * p.g + e : i * p.g + e + 1, :]
            lowdin_out[i, e] = (value[:, e * b : (e + 1) * b] * m).astype(jnp.bfloat16)


def outputs(p, next_rows, sums, root_both, hamilton):
    b = p.b
    out = jax.ShapeDtypeStruct((p.n, p.g, b, b), jnp.bfloat16)
    return pl.pallas_call(
        functools.partial(outputs_kernel, p),
        out_shape=(out, out, out),
        in_specs=vmem(5 + len(hamilton)),
        out_specs=tuple(vmem(3)),
        scratch_shapes=[pltpu.VMEM((3 * p.n * b, p.width * b), jnp.bfloat16)],
        compiler_params=params(),
        name="outputs",
    )(next_rows, *sums, root_both, *hamilton)


def join_kernel(p, ready, own_ref, partner_ref, *refs):
    b = p.b
    rows = lax.broadcasted_iota(jnp.int32, (p.mask_rows, b), 0)
    if ready:
        partner_mask, out_ref = refs
        out_ref[0] = own_ref[...]
        parts = ((1, partner_ref, partner_mask),)
    else:
        own_mask, partner_mask, out_ref = refs
        parts = ((0, own_ref, own_mask), (1, partner_ref, partner_mask))
    for half, x_ref, mask_ref in parts:
        marks = jnp.zeros((p.mask_rows, b), jnp.float32)
        for r in range(p.n):
            for e in range(p.g):
                m = (mask_ref[e, r] > 0).astype(jnp.float32)
                marks = jnp.where(rows == r * p.g + e, m, marks)
                value = (x_ref[r, e].astype(jnp.float32) * m).astype(jnp.bfloat16)
                block = pl.ds((r * p.g + e) * b, b)
                out_ref[half, block, :] = value
        out_ref[half, p.n * p.g * b :, :] = marks.astype(jnp.bfloat16)


def join(p, own, partner, own_mask, partner_mask):
    ready = own_mask is None
    masks = (partner_mask,) if ready else (own_mask, partner_mask)
    return pl.pallas_call(
        functools.partial(join_kernel, p, ready),
        out_shape=jax.ShapeDtypeStruct((2, p.unit, p.b), jnp.bfloat16),
        in_specs=vmem(2) + smem(len(masks)),
        out_specs=vmem(1)[0],
        compiler_params=params(),
        name="join",
    )(own, partner, *masks)


def body(root_margin, inverse_root, hamiltonian, margin_mask, hamilton_mask):
    rows, group, block = root_margin.shape[0], root_margin.shape[1], root_margin.shape[2]
    groups, cannon = lax.axis_size("rep"), lax.axis_size("cannon")
    p = Plan(rows, group, groups, block, cannon)

    def relay_route(step):
        route = []
        for c in range(cannon):
            for z in range(groups):
                sign = 1 - 2 * (c % 2)
                if 0 <= z - sign * (step - 1) < groups and 0 <= z + sign < groups:
                    route.append((c * groups + z, c * groups + z + sign))
        return route

    def direct_route(distance):
        route = []
        for c in range(cannon):
            for z in range(groups):
                to = z + distance * (1 - 2 * (c % 2))
                if 0 <= to < groups:
                    route.append((c * groups + z, c * groups + to))
        return route

    aside_route = [(c, c ^ 1) for c in range(cannon)]
    across_route = [(c, (c + 1) % cannon if c % 2 else (c - 1) % cannon) for c in range(cannon)]

    def relay(x, step):
        return lax.ppermute(x, AXES, relay_route(step))

    def aside(x):
        return lax.ppermute(x, "cannon", aside_route)

    def across(x):
        return lax.ppermute(x, "cannon", across_route)

    everything = list(range(1, p.steps + 1))
    root_parts = p.halo_parts([[s] for s in everything])
    inverse_parts = p.halo_parts([[0, 1]] + [[s] for s in everything[1:]])
    own_mask = margin_mask.T
    partner_mask = aside(own_mask)
    pieces = []
    alone = prep(p, root_margin, margin_mask)
    root_beyond = across(alone)
    for name, x in (("r", root_margin), ("i", inverse_root)):
        partner = aside(x)
        if name == "r":
            both = join(p, alone, partner, None, partner_mask)
        else:
            both = join(p, x, partner, own_mask, partner_mask)
        held, swapped = [], []
        step = both
        for s in everything:
            step = relay(step, s)
            held.append(step)
            swapped.append(aside(step))
        pieces.append((both, held, swapped))
    root, inverse = pieces

    own = prep(p, hamiltonian, hamilton_mask)
    partner = aside(own)
    beyond = across(own)
    beside = aside(beyond)
    near = pack_near(p, own, partner, beside)
    held, swapped = [], []
    for s, message in enumerate(near, 1):
        held.append(lax.ppermute(message, AXES, direct_route(s)))
        swapped.append(aside(held[-1]))
    hamilton = (own, partner, beyond, *held, *swapped)

    root_messages = []
    for s, lists in zip(everything, root_parts):
        message = pack(p, root, everything[:s], False, lists)
        root_messages.append(across(message))
    inverse_messages = []
    for s, lists in zip(everything, inverse_parts):
        message = pack(p, inverse, everything[:s], True, lists)
        inverse_messages.append(across(message))
    tables = [p.dense_targets(lists) for lists in root_parts[:-1]]
    main, left, reach, marks = polynomial_main(
        p, tables, root_messages[:-1], root_beyond, root, inverse
    )
    poly, own_sum, across_sum, aside_sum = polynomial(
        p, (p.band_targets(root_parts[-1]), p.reach_targets(root_parts[-1])), root_messages[-1], main, left, reach, marks
    )
    across_sum = across(across_sum)
    aside_sum = aside(aside_sum)
    main = inverse_main(p, poly, inverse)
    inverse_tables = [p.band_targets(lists) for lists in inverse_parts]
    next_rows = inverse_rows(p, inverse_tables, poly, main, marks, inverse_messages)
    results = outputs(p, next_rows, (own_sum, across_sum, aside_sum), root[0], hamilton)
    return results


def solution(mesh):
    blocks = P("cannon", "rep", None, None)
    masks = P("cannon", "rep")
    return jax.shard_map(
        body,
        mesh=mesh,
        in_specs=(blocks, blocks, blocks, masks, masks),
        out_specs=(blocks, blocks, blocks),
        check_vma=False,
    )
```
